256 devices in a mesh: plane: 2 (over core), row: 8 (over z), col: 16 (over y, x).
Axes of the slice: x: 4, y: 4, z: 8, core: 2. Of those that a mesh axis runs over, the one named last changes fastest.
Arguments:
- velocity: float32 [3, 4, 4096, 4096], P(None, 'plane', 'row', 'col'), may hold values from -60 to 60
Outputs:
- dissipation: float32 [4, 4096, 4096], P('plane', 'row', 'col')
- fine_means: float32 [128, 128], P('row', 'col')
- coarse_means: float32 [4, 4], replicated
The draws below stay inside these ranges and needn't reach their ends.
All inputs are finite; a program needn't handle non-finite values.
Results may differ from the reference program's by a relative error of at most 0.000078.
Values sent between devices are 32-bit elements; how exact they have to be, the bound alone decides.
No kernel may reach another device: no remote copies, remote signals or barrier semaphores. Data moves between devices by JAX's collectives and lax.ppermute only.
A program may use at most 128 MiB of HBM per device.

```python
import math
import jax
import jax.numpy as jnp

N = 4096
FINE = 32
COARSE = 1024
NZ = 4


def draw_velocity(key, part):
    base_key = jax.random.fold_in(key, 7)
    subkeys = jax.random.split(base_key, 4)
    full_shape = (3, NZ, N, N)
    noise_vals = jnp.clip(jax.random.normal(subkeys[0], full_shape, jnp.float32), -5.0, 5.0)
    row_scale = jnp.exp(jax.random.uniform(subkeys[1], (N,), jnp.float32, -1.15, 1.15))
    col_scale = jnp.exp(jax.random.uniform(subkeys[2], (N,), jnp.float32, -1.15, 1.15))
    plane_scale = jnp.exp(jax.random.uniform(subkeys[3], (NZ,), jnp.float32, -0.5, 0.5))
    position = jnp.arange(N).astype(jnp.float32) / N
    plane_pos = jnp.arange(NZ).astype(jnp.float32) / NZ
    rise_fac = jnp.exp(0.5 * math.log(3.0) * position)
    amplitude = 0.12 * (plane_scale * jnp.exp(0.55 * plane_pos))[:, None, None]
    amplitude = amplitude * (row_scale * rise_fac)[None, :, None] * (col_scale * rise_fac)[None, None, :]
    values = noise_vals * amplitude[None]
    return values


def setup_inputs(seed: int = 0) -> dict:
    seeds = jax.random.split(jax.random.key(seed), 2)
    return {
        "velocity": draw_velocity(jax.random.fold_in(seeds[1], 71), 0),
    }


def wave_numbers(length):
    indices = jnp.arange(length)
    signed = jnp.where(indices < length // 2, indices, indices - length)
    signed = jnp.where(indices == length // 2, 0, signed)
    return signed.astype(jnp.float32) * (2.0 * math.pi / length)


def derivative(values, along):
    length = values.shape[along]
    wavenum = wave_numbers(length)
    if along == 1:
        wavenum = wavenum.reshape(length, 1)
    spectrum = jnp.fft.fft(values, axis=along)
    return jnp.real(jnp.fft.ifft(spectrum * (1j * wavenum), axis=along)).astype(jnp.float32)


def z_diff(values):
    return (jnp.roll(values, -1, axis=0) - jnp.roll(values, 1, axis=0)) * 0.5


def box_means(dissip, edge):
    planes = dissip.shape[0]
    count = dissip.shape[1] // edge
    column_sum = jnp.sum(dissip, axis=0)
    boxed = column_sum.reshape(count, edge, count, edge).sum(axis=(1, 3))
    return boxed * (1.0 / (planes * edge * edge))


def reference(velocity):
    vel_u = velocity[0]
    vel_v = velocity[1]
    vel_w = velocity[2]
    single = derivative(vel_u, 1)
    dissip = single * single
    single = derivative(vel_v, 2)
    dissip = dissip + single * single
    single = z_diff(vel_w)
    dissip = dissip + single * single
    cross_sum = derivative(vel_u, 2) + derivative(vel_v, 1)
    dissip = dissip + 0.5 * cross_sum * cross_sum
    cross_sum = z_diff(vel_u) + derivative(vel_w, 1)
    dissip = dissip + 0.5 * cross_sum * cross_sum
    cross_sum = z_diff(vel_v) + derivative(vel_w, 2)
    dissip = dissip + 0.5 * cross_sum * cross_sum
    return dissip, box_means(dissip, FINE), box_means(dissip, COARSE)
```

```python
import functools
import math

import jax
import jax.numpy as jnp
import numpy as np
from jax import lax
from jax.experimental import pallas as pl
from jax.experimental.pallas import tpu as pltpu
from jax.sharding import Mesh
from jax.sharding import PartitionSpec as P

N = 4096
FINE = 32
COARSE = 1024
M = 256
ROWS = 8
DISTANCES = (4, 3, 5, 2, 6, 1, 7)
COL = ("col_0", "col_1")
PLANE_COL = ("plane", "col_0", "col_1")
HIGH = lax.Precision.HIGHEST


def toeplitz_parts():
    lags = np.arange(M)[:, None] - np.arange(M)[None, :]
    off = lags != 0
    base = np.zeros((M, M))
    base[off] = (1.0 / 16) * (math.pi / M) * (-1.0) ** lags[off] / np.sin(math.pi * lags[off] / M)
    turn = 2.0 * math.pi / N * (np.arange(16) - 8)[:, None] * np.arange(M)[None, :]
    cos_r, sin_r = np.cos(turn), np.sin(turn)
    cos_c = np.zeros((M, 128))
    sin_c = np.zeros((M, 128))
    cos_c[:, :16] = cos_r.T
    sin_c[:, :16] = sin_r.T
    return [np.asarray(a, np.float32) for a in (base, cos_r, sin_r, cos_c, sin_c)]


def table_kernel(base, cos_r, sin_r, cos_c, sin_c, out):
    left = lax.broadcasted_iota(jnp.int32, (M, M), 0)
    right = lax.broadcasted_iota(jnp.int32, (M, M), 1)
    for k in range(9):
        ca, sa = cos_c[:, k : k + 1], sin_c[:, k : k + 1]
        cb, sb = cos_r[k : k + 1, :], sin_r[k : k + 1, :]
        out[k] = base[...] * (ca * cb + sa * sb)
        if 0 < k < 8:
            middle = 2.0 * math.pi / N * (k - 8) / 16
            out[8 + k] = base[...] * (sa * cb - ca * sb) + jnp.where(left == right, middle, 0.0)


def vmem_call(kernel, outs, scratch=(), smem=0):
    def call(*args):
        specs = [pl.BlockSpec(memory_space=pltpu.SMEM)] * smem
        specs += [pl.BlockSpec(memory_space=pltpu.VMEM)] * (len(args) - smem)
        many = isinstance(outs, (list, tuple))
        out_specs = jax.tree.map(lambda _: pl.BlockSpec(memory_space=pltpu.VMEM), list(outs) if many else outs)
        return pl.pallas_call(
            kernel,
            out_shape=list(outs) if many else outs,
            in_specs=specs,
            out_specs=out_specs,
            scratch_shapes=list(scratch),
        )(*args)

    return call


def f32(*shape):
    return jax.ShapeDtypeStruct(shape, jnp.float32)


def real_dft(values):
    n = len(values)
    if n == 2:
        return [(values[0] + values[1], None), (values[0] - values[1], None)]
    even, odd = real_dft(values[0::2]), real_dft(values[1::2])
    half = n // 2
    out = [None] * (half + 1)
    out[0] = (even[0][0] + odd[0][0], None)
    out[half] = (even[0][0] - odd[0][0], None)
    for k in range(1, n // 4):
        angle = 2.0 * math.pi * k / n
        c, s = math.cos(angle), math.sin(angle)
        (er, ei), (orr, oi) = even[k], odd[k]
        if 2 * k * 4 == n:
            tr, ti = (orr + oi) * c, (oi - orr) * c
        else:
            tr, ti = orr * c + oi * s, oi * c - orr * s
        out[k] = (er + tr, ei + ti)
        out[half - k] = (er - tr, ti - ei)
    q = n // 4
    out[q] = (even[q][0], -odd[q][0])
    return out


def real_idft(spec):
    half = len(spec) - 1
    n = 2 * half
    if n == 2:
        return [spec[0][0] + spec[1][0], spec[0][0] - spec[1][0]]
    q = n // 4
    even, odd = [None] * (q + 1), [None] * (q + 1)
    even[0] = (spec[0][0] + spec[half][0], None)
    odd[0] = (spec[0][0] - spec[half][0], None)
    even[q] = (2.0 * spec[q][0], None)
    odd[q] = (-2.0 * spec[q][1], None)
    for k in range(1, q):
        angle = 2.0 * math.pi * k / n
        c, s = math.cos(angle), math.sin(angle)
        (ar, ai), (br, bi) = spec[k], spec[half - k]
        even[k] = (ar + br, ai - bi)
        dr, di = ar - br, ai + bi
        if 8 * k == n:
            odd[k] = ((dr - di) * c, (dr + di) * c)
        else:
            odd[k] = (dr * c - di * s, dr * s + di * c)
    out = [None] * n
    out[0::2] = real_idft(even)
    out[1::2] = real_idft(odd)
    return out


def lane_ids(rows):
    return lax.broadcasted_iota(jnp.int32, (rows, 128), 1)


def swap_lanes(four):
    group = lax.broadcasted_iota(jnp.int32, four[0].shape, 1) // 32
    low, even = group < 2, lax.rem(group, 2) == 0
    a, b, c, d = four
    a, c = jnp.where(low, a, pltpu.roll(c, 64, 1)), jnp.where(low, pltpu.roll(a, 64, 1), c)
    b, d = jnp.where(low, b, pltpu.roll(d, 64, 1)), jnp.where(low, pltpu.roll(b, 64, 1), d)
    a, b = jnp.where(even, a, pltpu.roll(b, 32, 1)), jnp.where(even, pltpu.roll(a, 96, 1), b)
    c, d = jnp.where(even, c, pltpu.roll(d, 32, 1)), jnp.where(even, pltpu.roll(c, 96, 1), d)
    return a, b, c, d


def pack_rows_kernel(row, *refs, count, step=32):
    vels, outs, held = refs[:count], refs[count : count + 8], refs[count + 8]

    def body(i, carry):
        rows = pl.ds(pl.multiple_of(i * step, step), step)
        later = pl.ds(pl.multiple_of(i * step + 256, step), step)
        for n, vel in enumerate(vels):
            for t in range(2):
                lanes = pl.ds(t * 128, 128)
                four = swap_lanes([vel[0, p, r, lanes] for r in (rows, later) for p in range(2)])
                for off in range(4):
                    held[4 * t + off, n, rows, :] = four[off]
        return carry

    lax.fori_loop(0, 256 // step, body, 0)
    for dist in range(ROWS):
        outs[dist][...] = held[lax.rem(row[0] + dist, ROWS)]


def pack_rows(row, velocity, comps):
    count = len(comps)
    whole = pl.BlockSpec((count, 256, 128), lambda i: (0, 0, 0))

    def one(c):
        return pl.BlockSpec((1, 2, 512, 256), lambda i: (c, 0, 0, 0))

    return pl.pallas_call(
        functools.partial(pack_rows_kernel, count=count),
        out_shape=[f32(count, 256, 128)] * ROWS,
        grid=(1,),
        in_specs=[pl.BlockSpec(memory_space=pltpu.SMEM)] + [one(c) for c in comps],
        out_specs=[whole] * ROWS,
        scratch_shapes=[pltpu.VMEM((ROWS, count, 256, 128), jnp.float32)],
        name="pack_rows",
    )(row, *([velocity] * count))


def hold_blocks(row, blocks, held):
    for dist in range(ROWS):
        held[lax.rem(row[0] + dist, ROWS)] = blocks[dist][0]


def home_tiles(held, rows, t):
    four = swap_lanes([held[4 * t + off, rows, :] for off in range(4)])
    return {(half, p): four[2 * half + p] for half in range(2) for p in range(2)}


def send_blocks(blocks):
    got = [blocks[0]] + [None] * (ROWS - 1)
    for dist in DISTANCES:
        perm = [(i, (i + dist) % ROWS) for i in range(ROWS)]
        got[(ROWS - dist) % ROWS] = lax.ppermute(blocks[dist], "row", perm)
    return got


def spectral_x(table, spec, res):
    res[0, :, :128] = jnp.dot(table[0], spec[0, :, :128], precision=HIGH)
    res[0, :, 128:] = jnp.dot(table[8], spec[0, :, 128:], precision=HIGH)

    def body(k, carry):
        a = jnp.dot(table[k], spec[k], precision=HIGH)
        b = jnp.dot(table[8 + k], spec[k], precision=HIGH)
        res[k, :, :128] = a[:, :128] - b[:, 128:]
        res[k, :, 128:] = a[:, 128:] + b[:, :128]
        return carry

    lax.fori_loop(1, 8, body, 0)


STEP = 16


def store_spec(spec, freq, rows):
    for k in range(8):
        re, im = freq[k]
        spec[k, rows, :128] = re
        spec[k, rows, 128:] = freq[8][0] if k == 0 else im


def load_spec(res, rows):
    freq = [(res[k, rows, :128], res[k, rows, 128:]) for k in range(8)]
    return [(freq[0][0], None)] + freq[1:] + [(freq[0][1], None)]


def grad_v_kernel(table, *refs):
    blocks, outs, spec, res = refs[:8], refs[8:16], refs[16], refs[17]
    low = lane_ids(STEP) < 64

    def forward(i, carry):
        rows = pl.ds(pl.multiple_of(i * STEP, STEP), STEP)
        values = []
        for j in range(8):
            src = blocks[j][0, rows, :]
            values += [src, pltpu.roll(src, 64, 1)]
        store_spec(spec, real_dft(values), rows)
        return carry

    lax.fori_loop(0, 256 // STEP, forward, 0)
    spectral_x(table, spec, res)

    def backward(i, carry):
        rows = pl.ds(pl.multiple_of(i * STEP, STEP), STEP)
        values = real_idft(load_spec(res, rows))
        for j in range(8):
            outs[j][0, rows, :] = jnp.where(low, values[2 * j], pltpu.roll(values[2 * j + 1], 64, 1))
        return carry

    lax.fori_loop(0, 256 // STEP, backward, 0)


X_SCRATCH = (pltpu.VMEM((8, 256, 256), jnp.float32), pltpu.VMEM((8, 256, 256), jnp.float32))


def grad_v(table, blocks):
    return vmem_call(grad_v_kernel, [f32(1, 256, 128)] * 8, X_SCRATCH)(table, *blocks)


def grad_uw_kernel(row, table, *refs):
    blocks, other, out, sums, spec, res = refs[:8], refs[8:16], refs[16], refs[17], refs[18], refs[19]
    lane = lane_ids(STEP)
    low = lane < 64
    first = lax.rem(lane // 32, 2) == 0

    def forward(i, carry):
        rows = pl.ds(pl.multiple_of(i * STEP, STEP), STEP)
        values = []
        for j in range(8):
            u, w = blocks[j][0, rows, :], blocks[j][1, rows, :]
            values += [jnp.where(low, u, pltpu.roll(w, 64, 1)), jnp.where(low, pltpu.roll(u, 64, 1), w)]
        store_spec(spec, real_dft(values), rows)
        return carry

    lax.fori_loop(0, 256 // STEP, forward, 0)
    spectral_x(table, spec, res)

    def backward(i, carry):
        rows = pl.ds(pl.multiple_of(i * STEP, STEP), STEP)
        values = real_idft(load_spec(res, rows))
        totals = []
        for j in range(8):
            a, b = values[2 * j], values[2 * j + 1]
            u_x = jnp.where(low, a, pltpu.roll(b, 64, 1))
            w_x = jnp.where(low, pltpu.roll(a, 64, 1), b)
            diff = blocks[j][0, rows, :] - other[j][0, rows, :]
            u_z = 0.5 * jnp.where(first, pltpu.roll(diff, 96, 1), -pltpu.roll(diff, 32, 1))
            cross = u_z + w_x
            part = u_x * u_x + 0.5 * (cross * cross)
            out[lax.rem(row[0] + j, ROWS), rows, :] = part
            totals.append(carry[j] + part)
        return tuple(totals)

    zero = jnp.zeros((STEP, 128), jnp.float32)
    totals = lax.fori_loop(0, 256 // STEP, backward, (zero,) * 8)
    for j in range(8):
        sums[j : j + 1, :] = jnp.sum(totals[j], axis=0, keepdims=True)


def grad_uw(row, table, other, blocks):
    outs = [f32(8, 256, 128), f32(8, 128)]
    return vmem_call(grad_uw_kernel, outs, X_SCRATCH, smem=1)(row, table, *blocks, *other)


def grad_y_kernel(table, data, out, spec, res):
    def forward(i, carry):
        c = i // 16
        k = lax.rem(i // 8, 2)
        p = lax.rem(i // 4, 2)
        half = pl.ds(pl.multiple_of(lax.rem(i // 2, 2) * 8, 8), 8)
        lanes = pl.ds(pl.multiple_of(lax.rem(i, 2) * 128, 128), 128)
        rows = pl.multiple_of((i // 2) * 8, 8)
        freq = real_dft([data[k, b, c, p, half, lanes] for b in range(16)])
        for f in range(8):
            spec[f, pl.ds(rows, 8), lanes] = freq[f][0]
            spec[f, pl.ds(rows + 192, 8), lanes] = freq[8][0] if f == 0 else freq[f][1]
        return carry

    lax.fori_loop(0, 48, forward, 0)
    res[0, :192] = jnp.dot(spec[0, :192], table[0], precision=HIGH) * -1.0
    res[0, 192:] = jnp.dot(spec[0, 192:], table[8], precision=HIGH) * -1.0

    def middle(f, carry):
        a = jnp.dot(spec[f], table[f], precision=HIGH)
        b = jnp.dot(spec[f], table[8 + f], precision=HIGH)
        res[f, :192] = -a[:192] - b[192:]
        res[f, 192:] = b[:192] - a[192:]
        return carry

    lax.fori_loop(1, 8, middle, 0)

    def backward(i, carry):
        k = i // 4
        half = pl.ds(pl.multiple_of(lax.rem(i // 2, 2) * 8, 8), 8)
        lanes = pl.ds(pl.multiple_of(lax.rem(i, 2) * 128, 128), 128)
        for p in range(2):

            def slope(c):
                start = pl.multiple_of(c * 64 + k * 32 + p * 16 + lax.rem(i // 2, 2) * 8, 8)
                freq = [(res[f, pl.ds(start, 8), lanes], res[f, pl.ds(start + 192, 8), lanes]) for f in range(8)]
                return real_idft([(freq[0][0], None)] + freq[1:] + [(freq[0][1], None)])

            def slope_z(c, b):
                gap = data[k, b, c, 1 - p, half, lanes] - data[1 - k, b, c, 1 - p, half, lanes]
                return gap * (0.5 if p == 0 else -0.5)

            for b, value in enumerate(slope(0)):
                out[k, b, 1, p, half, lanes] = value
            for b, value in enumerate(slope(1)):
                w_z = slope_z(2, b)
                out[k, b, 0, p, half, lanes] = value * value + w_z * w_z
            for b, value in enumerate(slope(2)):
                cross = slope_z(1, b) + value
                out[k, b, 0, p, half, lanes] += 0.5 * (cross * cross)
        return carry

    lax.fori_loop(0, 8, backward, 0)


def grad_y(table, data):
    scratch = (pltpu.VMEM((8, 384, 256), jnp.float32), pltpu.VMEM((8, 384, 256), jnp.float32))
    return vmem_call(grad_y_kernel, f32(2, 16, 2, 2, 16, 256), scratch)(table, data)


def pack_cols_kernel(vel, out):
    def body(g, carry):
        start = pl.multiple_of(g * 16, 16)
        for c in range(3):
            for p in range(2):
                out[g, c, p] = vel[c, p, pl.ds(start, 16), :]
        return carry

    lax.fori_loop(0, 32, body, 0)


def partial_kernel(place, y_terms, x_sums, *refs):
    blocks, out, boxes, held = refs[:8], refs[8], refs[9], refs[10]
    hold_blocks(place, blocks, held)

    def body(i, carry):
        rows = pl.ds(pl.multiple_of(i * 16, 16), 16)
        for t in range(2):
            lanes = pl.ds(t * 128, 128)
            for (half, p), v_x in home_tiles(held, rows, t).items():
                g = i + 16 * half
                cross = y_terms[g, 1, p, :, lanes] + v_x
                value = y_terms[g, 0, p, :, lanes] + 0.5 * (cross * cross)
                out[p, pl.ds(pl.multiple_of(g * 16, 16), 16), lanes] = value
                carry = carry + value
        return carry

    total = lax.fori_loop(0, 16, body, jnp.zeros((16, 128), jnp.float32))
    down = lax.broadcasted_iota(jnp.int32, (8, 128), 0)
    mine = lax.broadcasted_iota(jnp.int32, (8, 128), 1) == place[1] // 4
    zero = jnp.zeros((8, 128), jnp.float32)
    found = jnp.where(down == place[0] // 2, jnp.sum(total), zero)
    for j in range(ROWS):
        box = lax.rem(place[0] + j, ROWS) // 2
        found = found + jnp.where(down == box, jnp.sum(x_sums[j : j + 1, :]), zero)
    boxes[...] = jnp.where(mine, found * (1.0 / (4 * COARSE * COARSE)), zero)


def final_kernel(part, select, held, out, boxes, lines):

    def body(a, carry):
        rows = pl.ds(pl.multiple_of(a * 32, 32), 32)
        for t in range(2):
            lanes = pl.ds(t * 128, 128)
            tiles = home_tiles(held, rows, t)
            for half in range(2):
                there = pl.ds(pl.multiple_of(a * 32 + 256 * half, 32), 32)
                first = part[0, there, lanes] + tiles[half, 0]
                second = part[1, there, lanes] + tiles[half, 1]
                out[0, there, lanes] = first
                out[1, there, lanes] = second
                total = (first + second).reshape(4, 8, 128).sum(axis=0)
                lines[a + 8 * half, :, lanes] = total
        return carry

    lax.fori_loop(0, 8, body, 0)
    boxes[...] = jnp.dot(jnp.sum(lines[...], axis=1), select[...], precision=HIGH)


def whole_step(velocity):
    row = lax.axis_index("row")
    col = lax.axis_index(COL)
    row_arg = row.astype(jnp.int32).reshape(1)
    parts = [jnp.asarray(a) for a in toeplitz_parts()]
    for_cols = vmem_call(pack_cols_kernel, f32(32, 3, 2, 16, 256))(velocity)
    lines = lax.all_to_all(for_cols, PLANE_COL, split_axis=0, concat_axis=0, tiled=True)
    v_blocks = pack_rows(row_arg, velocity, (1,))
    v_blocks = send_blocks(v_blocks)
    uw_blocks = pack_rows(row_arg, velocity, (0, 2))
    uw_blocks = send_blocks(uw_blocks)
    table = vmem_call(table_kernel, f32(16, M, M))(*parts)
    v_x = grad_v(table, v_blocks)
    v_x = send_blocks(v_x)
    y_terms = grad_y(table, lines.reshape(2, 16, 3, 2, 16, 256))
    y_terms = lax.all_to_all(
        y_terms.reshape(32, 2, 2, 16, 256), PLANE_COL, split_axis=0, concat_axis=0, tiled=True
    )
    other = [lax.ppermute(b, "plane", [(0, 1), (1, 0)]) for b in uw_blocks]
    x_terms, x_sums = grad_uw(row_arg, table, other, uw_blocks)
    x_terms = lax.all_to_all(x_terms, "row", split_axis=0, concat_axis=0, tiled=True)
    held = pltpu.VMEM((ROWS, 256, 128), jnp.float32)
    place = jnp.stack([row, col]).astype(jnp.int32)
    part, coarse = vmem_call(partial_kernel, [f32(2, 512, 256), f32(8, 128)], (held,), smem=1)(
        place, y_terms, x_sums, *v_x
    )
    coarse = sum_of_four(coarse, ("plane", "row"), lambda i, n: i ^ (8, 1, 9)[n])
    coarse = sum_of_four(coarse, "row", lambda i, n: (i + (4, 2, 6)[n]) % 8)
    coarse = sum_of_four(coarse, "col_1", lambda i, n: (i + (2, 1, 3)[n]) % 4)
    coarse = sum_of_four(coarse, "col_0", lambda i, n: (i + (2, 1, 3)[n]) % 4)
    coarse = coarse[:4, :4]
    select = np.zeros((256, 128), np.float32)
    select[np.arange(256), np.arange(256) // FINE] = 1.0 / (4 * FINE * FINE)
    coarse, part = lax.optimization_barrier((coarse, part))
    dissip, fine = vmem_call(
        final_kernel,
        [f32(2, 512, 256), f32(16, 128)],
        (pltpu.VMEM((16, 8, 256), jnp.float32),),
    )(part, jnp.asarray(select), x_terms)
    fine = (fine + lax.ppermute(fine, "plane", [(0, 1), (1, 0)]))[:, :8]
    return dissip, fine, coarse


def sum_of_four(values, axis, partner):
    size = lax.axis_size(axis)
    got = [lax.ppermute(values, axis, [(i, partner(i, n)) for i in range(size)]) for n in range(3)]
    return (values + got[0]) + (got[1] + got[2])


def solution(mesh):
    split = Mesh(
        mesh.devices.reshape(mesh.shape["plane"], mesh.shape["row"], 4, 4),
        ("plane", "row", "col_0", "col_1"),
    )
    in_specs = (P(None, "plane", "row", COL),)
    out_specs = (P("plane", "row", COL), P("row", COL), P())
    return jax.shard_map(whole_step, mesh=split, in_specs=in_specs, out_specs=out_specs, check_vma=False)
```

```python
import functools
import math

import jax
import jax.numpy as jnp
import numpy as np
from jax import lax
from jax.experimental import pallas as pl
from jax.experimental.pallas import tpu as pltpu
from jax.sharding import Mesh
from jax.sharding import PartitionSpec as P

N = 4096
FINE = 32
COARSE = 1024
M = 256
ROWS = 8
DISTANCES = (4, 3, 5, 2, 6, 1, 7)
COL = ("col_0", "col_1")
PLANE_COL = ("plane", "col_0", "col_1")
HIGH = lax.Precision.HIGHEST


def turns():
    turn = 2.0 * math.pi / N * (np.arange(16) - 8)[:, None] * np.arange(M)[None, :]
    tall = np.zeros((2, M, 128), np.float32)
    tall[0, :, :16] = np.cos(turn).T
    tall[1, :, :16] = np.sin(turn).T
    return np.stack([np.cos(turn), np.sin(turn)]).astype(np.float32), tall


def table_kernel(wide, tall, out, base):
    left = lax.broadcasted_iota(jnp.int32, (M, M), 0)
    right = lax.broadcasted_iota(jnp.int32, (M, M), 1)
    lag = left - right
    size = jnp.abs(lag)
    angle = jnp.minimum(size, M - size).astype(jnp.float32) * (math.pi / M)
    scale = jnp.where((lag > 0) == (lax.rem(size, 2) == 0), math.pi / (16 * M), -math.pi / (16 * M))
    base[...] = jnp.where(lag == 0, 0.0, scale / jnp.where(lag == 0, 1.0, jnp.sin(angle)))
    for k in range(9):
        ca, sa = tall[0, :, k : k + 1], tall[1, :, k : k + 1]
        cb, sb = wide[0, k : k + 1, :], wide[1, k : k + 1, :]
        out[k] = base[...] * (ca * cb + sa * sb)
        if 0 < k < 8:
            middle = 2.0 * math.pi / N * (k - 8) / 16
            out[8 + k] = base[...] * (sa * cb - ca * sb) + jnp.where(left == right, middle, 0.0)


def vmem_call(kernel, outs, scratch=(), smem=0):
    def call(*args):
        specs = [pl.BlockSpec(memory_space=pltpu.SMEM)] * smem
        specs += [pl.BlockSpec(memory_space=pltpu.VMEM)] * (len(args) - smem)
        many = isinstance(outs, (list, tuple))
        out_specs = jax.tree.map(lambda _: pl.BlockSpec(memory_space=pltpu.VMEM), list(outs) if many else outs)
        return pl.pallas_call(
            kernel,
            out_shape=list(outs) if many else outs,
            in_specs=specs,
            out_specs=out_specs,
            scratch_shapes=list(scratch),
        )(*args)

    return call


def f32(*shape):
    return jax.ShapeDtypeStruct(shape, jnp.float32)


def real_dft(values):
    n = len(values)
    if n == 2:
        return [(values[0] + values[1], None), (values[0] - values[1], None)]
    even, odd = real_dft(values[0::2]), real_dft(values[1::2])
    half = n // 2
    out = [None] * (half + 1)
    out[0] = (even[0][0] + odd[0][0], None)
    out[half] = (even[0][0] - odd[0][0], None)
    for k in range(1, n // 4):
        angle = 2.0 * math.pi * k / n
        c, s = math.cos(angle), math.sin(angle)
        (er, ei), (orr, oi) = even[k], odd[k]
        if 2 * k * 4 == n:
            tr, ti = (orr + oi) * c, (oi - orr) * c
        else:
            tr, ti = orr * c + oi * s, oi * c - orr * s
        out[k] = (er + tr, ei + ti)
        out[half - k] = (er - tr, ti - ei)
    q = n // 4
    out[q] = (even[q][0], -odd[q][0])
    return out


def real_idft(spec):
    half = len(spec) - 1
    n = 2 * half
    if n == 2:
        return [spec[0][0] + spec[1][0], spec[0][0] - spec[1][0]]
    q = n // 4
    even, odd = [None] * (q + 1), [None] * (q + 1)
    even[0] = (spec[0][0] + spec[half][0], None)
    odd[0] = (spec[0][0] - spec[half][0], None)
    even[q] = (2.0 * spec[q][0], None)
    odd[q] = (-2.0 * spec[q][1], None)
    for k in range(1, q):
        angle = 2.0 * math.pi * k / n
        c, s = math.cos(angle), math.sin(angle)
        (ar, ai), (br, bi) = spec[k], spec[half - k]
        even[k] = (ar + br, ai - bi)
        dr, di = ar - br, ai + bi
        if 8 * k == n:
            odd[k] = ((dr - di) * c, (dr + di) * c)
        else:
            odd[k] = (dr * c - di * s, dr * s + di * c)
    out = [None] * n
    out[0::2] = real_idft(even)
    out[1::2] = real_idft(odd)
    return out


def lane_ids(rows):
    return lax.broadcasted_iota(jnp.int32, (rows, 128), 1)


def swap_lanes(four):
    group = lax.broadcasted_iota(jnp.int32, four[0].shape, 1) // 32
    low, even = group < 2, lax.rem(group, 2) == 0
    a, b, c, d = four
    a, c = jnp.where(low, a, pltpu.roll(c, 64, 1)), jnp.where(low, pltpu.roll(a, 64, 1), c)
    b, d = jnp.where(low, b, pltpu.roll(d, 64, 1)), jnp.where(low, pltpu.roll(b, 64, 1), d)
    a, b = jnp.where(even, a, pltpu.roll(b, 32, 1)), jnp.where(even, pltpu.roll(a, 96, 1), b)
    c, d = jnp.where(even, c, pltpu.roll(d, 32, 1)), jnp.where(even, pltpu.roll(c, 96, 1), d)
    return a, b, c, d


def pack_rows_kernel(row, *refs, count, step=32):
    vels, outs, held = refs[:count], refs[count : count + 8], refs[count + 8]

    def body(i, carry):
        rows = pl.ds(pl.multiple_of(i * step, step), step)
        later = pl.ds(pl.multiple_of(i * step + 256, step), step)
        for n, vel in enumerate(vels):
            for t in range(2):
                lanes = pl.ds(t * 128, 128)
                four = swap_lanes([vel[0, p, r, lanes] for r in (rows, later) for p in range(2)])
                for off in range(4):
                    held[4 * t + off, n, rows, :] = four[off]
        return carry

    lax.fori_loop(0, 256 // step, body, 0)
    for dist in range(ROWS):
        outs[dist][...] = held[lax.rem(row[0] + dist, ROWS)]


def pack_rows(row, velocity, comps):
    count = len(comps)
    whole = pl.BlockSpec((count, 256, 128), lambda i: (0, 0, 0))

    def one(c):
        return pl.BlockSpec((1, 2, 512, 256), lambda i: (c, 0, 0, 0))

    return pl.pallas_call(
        functools.partial(pack_rows_kernel, count=count),
        out_shape=[f32(count, 256, 128)] * ROWS,
        grid=(1,),
        in_specs=[pl.BlockSpec(memory_space=pltpu.SMEM)] + [one(c) for c in comps],
        out_specs=[whole] * ROWS,
        scratch_shapes=[pltpu.VMEM((ROWS, count, 256, 128), jnp.float32)],
        name="pack_rows",
    )(row, *([velocity] * count))


def hold_blocks(row, blocks, held):
    for dist in range(ROWS):
        held[lax.rem(row[0] + dist, ROWS)] = blocks[dist][0]


def home_tiles(held, rows, t):
    four = swap_lanes([held[4 * t + off, rows, :] for off in range(4)])
    return {(half, p): four[2 * half + p] for half in range(2) for p in range(2)}


def send_blocks(blocks):
    got = [blocks[0]] + [None] * (ROWS - 1)
    for dist in DISTANCES:
        perm = [(i, (i + dist) % ROWS) for i in range(ROWS)]
        got[(ROWS - dist) % ROWS] = lax.ppermute(blocks[dist], "row", perm)
    return got


def spectral_x(table, spec, res):
    def body(k, carry):
        lone = k == 0
        a = jnp.dot(table[k], spec[k], precision=HIGH)
        b = jnp.dot(table[8 + k], spec[k], precision=HIGH)
        res[k, :, :128] = a[:, :128] - jnp.where(lone, 0.0, b[:, 128:])
        res[k, :, 128:] = jnp.where(lone, b[:, 128:], a[:, 128:] + b[:, :128])
        return carry

    lax.fori_loop(0, 8, body, 0)


STEP = 16


def store_spec(spec, freq, rows):
    for k in range(8):
        re, im = freq[k]
        spec[k, rows, :128] = re
        spec[k, rows, 128:] = freq[8][0] if k == 0 else im


def load_spec(res, rows):
    freq = [(res[k, rows, :128], res[k, rows, 128:]) for k in range(8)]
    return [(freq[0][0], None)] + freq[1:] + [(freq[0][1], None)]


def grad_v_kernel(table, *refs):
    blocks, outs, spec, res = refs[:8], refs[8:16], refs[16], refs[17]
    low = lane_ids(STEP) < 64

    def forward(i, carry):
        rows = pl.ds(pl.multiple_of(i * STEP, STEP), STEP)
        values = []
        for j in range(8):
            src = blocks[j][0, rows, :]
            values += [src, pltpu.roll(src, 64, 1)]
        store_spec(spec, real_dft(values), rows)
        return carry

    lax.fori_loop(0, 256 // STEP, forward, 0)
    spectral_x(table, spec, res)

    def backward(i, carry):
        rows = pl.ds(pl.multiple_of(i * STEP, STEP), STEP)
        values = real_idft(load_spec(res, rows))
        for j in range(8):
            outs[j][0, rows, :] = jnp.where(low, values[2 * j], pltpu.roll(values[2 * j + 1], 64, 1))
        return carry

    lax.fori_loop(0, 256 // STEP, backward, 0)


X_SCRATCH = (pltpu.VMEM((8, 256, 256), jnp.float32), pltpu.VMEM((8, 256, 256), jnp.float32))


def grad_v(table, blocks):
    return vmem_call(grad_v_kernel, [f32(1, 256, 128)] * 8, X_SCRATCH)(table, *blocks)


def stack_first_kernel(*refs):
    blocks, out, sems = refs[:8], refs[8], refs[9]
    copies = [pltpu.make_async_copy(blocks[j].at[0], out.at[j], sems.at[j]) for j in range(8)]
    for copy in copies:
        copy.start()
    for copy in copies:
        copy.wait()


def stack_first(blocks):
    anywhere = pl.BlockSpec(memory_space=pl.ANY)
    return pl.pallas_call(
        stack_first_kernel,
        out_shape=f32(8, 256, 128),
        in_specs=[anywhere] * 8,
        out_specs=anywhere,
        scratch_shapes=[pltpu.SemaphoreType.DMA((8,))],
        name="stack_first",
    )(*blocks)


def grad_uw_kernel(row, table, *refs):
    blocks, other, out, sums, spec, res = refs[:8], *refs[8:]
    lane = lane_ids(STEP)
    low = lane < 64
    first = lax.rem(lane // 32, 2) == 0

    def forward(i, carry):
        rows = pl.ds(pl.multiple_of(i * STEP, STEP), STEP)
        values = []
        for j in range(8):
            u, w = blocks[j][0, rows, :], blocks[j][1, rows, :]
            values += [jnp.where(low, u, pltpu.roll(w, 64, 1)), jnp.where(low, pltpu.roll(u, 64, 1), w)]
        store_spec(spec, real_dft(values), rows)
        return carry

    lax.fori_loop(0, 256 // STEP, forward, 0)
    spectral_x(table, spec, res)

    def backward(i, carry):
        rows = pl.ds(pl.multiple_of(i * STEP, STEP), STEP)
        values = real_idft(load_spec(res, rows))
        totals = []
        for j in range(8):
            a, b = values[2 * j], values[2 * j + 1]
            u_x = jnp.where(low, a, pltpu.roll(b, 64, 1))
            w_x = jnp.where(low, pltpu.roll(a, 64, 1), b)
            diff = blocks[j][0, rows, :] - other[j, rows, :]
            u_z = 0.5 * jnp.where(first, pltpu.roll(diff, 96, 1), -pltpu.roll(diff, 32, 1))
            cross = u_z + w_x
            part = u_x * u_x + 0.5 * (cross * cross)
            out[lax.rem(row[0] + j, ROWS), rows, :] = part
            totals.append(carry[j] + part)
        return tuple(totals)

    zero = jnp.zeros((STEP, 128), jnp.float32)
    totals = lax.fori_loop(0, 256 // STEP, backward, (zero,) * 8)
    for j in range(8):
        sums[j : j + 1, :] = jnp.sum(totals[j], axis=0, keepdims=True)


def grad_uw(row, table, other, blocks):
    outs = [f32(8, 256, 128), f32(8, 128)]
    return vmem_call(grad_uw_kernel, outs, X_SCRATCH, smem=1)(row, table, *blocks, other)


def grad_y_kernel(table, data, out, spec, res):
    def forward(i, carry):
        c = i // 16
        k = lax.rem(i // 8, 2)
        p = lax.rem(i // 4, 2)
        half = pl.ds(pl.multiple_of(lax.rem(i // 2, 2) * 8, 8), 8)
        lanes = pl.ds(pl.multiple_of(lax.rem(i, 2) * 128, 128), 128)
        rows = pl.multiple_of((i // 2) * 8, 8)
        freq = real_dft([data[k, b, c, p, half, lanes] for b in range(16)])
        for f in range(8):
            spec[f, pl.ds(rows, 8), lanes] = freq[f][0]
            spec[f, pl.ds(rows + 192, 8), lanes] = freq[8][0] if f == 0 else freq[f][1]
        return carry

    lax.fori_loop(0, 48, forward, 0)

    def middle(f, carry):
        lone = f == 0
        a = jnp.dot(spec[f], table[f], precision=HIGH)
        b = jnp.dot(spec[f], table[8 + f], precision=HIGH)
        res[f, :192] = -a[:192] - jnp.where(lone, 0.0, b[192:])
        res[f, 192:] = jnp.where(lone, -b[192:], b[:192] - a[192:])
        return carry

    lax.fori_loop(0, 8, middle, 0)

    def backward(i, carry):
        k = i // 4
        half = pl.ds(pl.multiple_of(lax.rem(i // 2, 2) * 8, 8), 8)
        lanes = pl.ds(pl.multiple_of(lax.rem(i, 2) * 128, 128), 128)
        for p in range(2):

            def slope(c):
                start = pl.multiple_of(c * 64 + k * 32 + p * 16 + lax.rem(i // 2, 2) * 8, 8)
                freq = [(res[f, pl.ds(start, 8), lanes], res[f, pl.ds(start + 192, 8), lanes]) for f in range(8)]
                return real_idft([(freq[0][0], None)] + freq[1:] + [(freq[0][1], None)])

            def slope_z(c, b):
                gap = data[k, b, c, 1 - p, half, lanes] - data[1 - k, b, c, 1 - p, half, lanes]
                return gap * (0.5 if p == 0 else -0.5)

            for b, value in enumerate(slope(0)):
                out[k, b, 1, p, half, lanes] = value
            for b, value in enumerate(slope(1)):
                w_z = slope_z(2, b)
                out[k, b, 0, p, half, lanes] = value * value + w_z * w_z
            for b, value in enumerate(slope(2)):
                cross = slope_z(1, b) + value
                out[k, b, 0, p, half, lanes] += 0.5 * (cross * cross)
        return carry

    lax.fori_loop(0, 8, backward, 0)


def grad_y(table, data):
    scratch = (pltpu.VMEM((8, 384, 256), jnp.float32), pltpu.VMEM((8, 384, 256), jnp.float32))
    return vmem_call(grad_y_kernel, f32(2, 16, 2, 2, 16, 256), scratch)(table, data)


def pack_cols_kernel(vel, out):
    def body(g, carry):
        start = pl.multiple_of(g * 16, 16)
        for c in range(3):
            for p in range(2):
                out[g, c, p] = vel[c, p, pl.ds(start, 16), :]
        return carry

    lax.fori_loop(0, 32, body, 0)


def partial_kernel(place, y_terms, x_sums, *refs):
    blocks, out, boxes, held = refs[:8], refs[8], refs[9], refs[10]
    hold_blocks(place, blocks, held)

    def body(i, carry):
        rows = pl.ds(pl.multiple_of(i * 16, 16), 16)
        for t in range(2):
            lanes = pl.ds(t * 128, 128)
            for (half, p), v_x in home_tiles(held, rows, t).items():
                g = i + 16 * half
                cross = y_terms[g, 1, p, :, lanes] + v_x
                value = y_terms[g, 0, p, :, lanes] + 0.5 * (cross * cross)
                out[p, pl.ds(pl.multiple_of(g * 16, 16), 16), lanes] = value
                carry = carry + value
        return carry

    total = lax.fori_loop(0, 16, body, jnp.zeros((16, 128), jnp.float32))
    down = lax.broadcasted_iota(jnp.int32, (8, 128), 0)
    mine = lax.broadcasted_iota(jnp.int32, (8, 128), 1) == place[1] // 4
    zero = jnp.zeros((8, 128), jnp.float32)
    found = jnp.where(down == place[0] // 2, jnp.sum(total), zero)
    for j in range(ROWS):
        box = lax.rem(place[0] + j, ROWS) // 2
        found = found + jnp.where(down == box, jnp.sum(x_sums[j : j + 1, :]), zero)
    boxes[...] = jnp.where(mine, found * (1.0 / (4 * COARSE * COARSE)), zero)


def final_kernel(part, held, out, boxes, lines):

    def body(a, carry):
        rows = pl.ds(pl.multiple_of(a * 32, 32), 32)
        for t in range(2):
            lanes = pl.ds(t * 128, 128)
            tiles = home_tiles(held, rows, t)
            for half in range(2):
                there = pl.ds(pl.multiple_of(a * 32 + 256 * half, 32), 32)
                first = part[0, there, lanes] + tiles[half, 0]
                second = part[1, there, lanes] + tiles[half, 1]
                out[0, there, lanes] = first
                out[1, there, lanes] = second
                total = (first + second).reshape(4, 8, 128).sum(axis=0)
                lines[a + 8 * half, :, lanes] = total
        return carry

    lax.fori_loop(0, 8, body, 0)
    cell = lax.broadcasted_iota(jnp.int32, (256, 128), 0) // FINE
    select = jnp.where(cell == lax.broadcasted_iota(jnp.int32, (256, 128), 1), 1.0 / (4 * FINE * FINE), 0.0)
    boxes[...] = jnp.dot(jnp.sum(lines[...], axis=1), select, precision=HIGH)


def whole_step(velocity):
    row = lax.axis_index("row")
    col = lax.axis_index(COL)
    row_arg = row.astype(jnp.int32).reshape(1)
    parts = [jnp.asarray(a) for a in turns()]
    for_cols = vmem_call(pack_cols_kernel, f32(32, 3, 2, 16, 256))(velocity)
    lines = lax.all_to_all(for_cols, PLANE_COL, split_axis=0, concat_axis=0, tiled=True)
    v_blocks = pack_rows(row_arg, velocity, (1,))
    v_blocks = send_blocks(v_blocks)
    uw_blocks = pack_rows(row_arg, velocity, (0, 2))
    uw_blocks = send_blocks(uw_blocks)
    table = vmem_call(table_kernel, f32(16, M, M), (pltpu.VMEM((M, M), jnp.float32),))(*parts)
    v_x = grad_v(table, v_blocks)
    v_x = send_blocks(v_x)
    y_terms = grad_y(table, lines.reshape(2, 16, 3, 2, 16, 256))
    y_terms = lax.all_to_all(
        y_terms.reshape(32, 2, 2, 16, 256), PLANE_COL, split_axis=0, concat_axis=0, tiled=True
    )
    other = stack_first(uw_blocks)
    other = lax.ppermute(other, "plane", [(0, 1), (1, 0)])
    x_terms, x_sums = grad_uw(row_arg, table, other, uw_blocks)
    x_terms = lax.all_to_all(x_terms, "row", split_axis=0, concat_axis=0, tiled=True)
    held = pltpu.VMEM((ROWS, 256, 128), jnp.float32)
    place = jnp.stack([row, col]).astype(jnp.int32)
    part, coarse = vmem_call(partial_kernel, [f32(2, 512, 256), f32(8, 128)], (held,), smem=1)(
        place, y_terms, x_sums, *v_x
    )
    coarse = sum_of_four(coarse, "col_1", lambda i, n: (i + (2, 1, 3)[n]) % 4)
    coarse = sum_of_four(coarse, "col_0", lambda i, n: (i + (2, 1, 3)[n]) % 4)
    coarse = sum_of_four(coarse, ("plane", "row"), lambda i, n: i ^ (8, 1, 9)[n])
    coarse = sum_of_four(coarse, "row", lambda i, n: (i + (4, 2, 6)[n]) % 8)
    coarse = coarse[:4, :4]
    dissip, fine = vmem_call(
        final_kernel,
        [f32(2, 512, 256), f32(16, 128)],
        (pltpu.VMEM((16, 8, 256), jnp.float32),),
    )(part, x_terms)
    fine = (fine + lax.ppermute(fine, "plane", [(0, 1), (1, 0)]))[:, :8]
    return dissip, fine, coarse


def sum_of_four(values, axis, partner):
    size = lax.axis_size(axis)
    got = [lax.ppermute(values, axis, [(i, partner(i, n)) for i in range(size)]) for n in range(3)]
    return (values + got[0]) + (got[1] + got[2])


def solution(mesh):
    split = Mesh(
        mesh.devices.reshape(mesh.shape["plane"], mesh.shape["row"], 4, 4),
        ("plane", "row", "col_0", "col_1"),
    )
    in_specs = (P(None, "plane", "row", COL),)
    out_specs = (P("plane", "row", COL), P("row", COL), P())
    return jax.shard_map(whole_step, mesh=split, in_specs=in_specs, out_specs=out_specs, check_vma=False)
```

```python
import functools
import math

import jax
import jax.numpy as jnp
import numpy as np
from jax import lax
from jax.experimental import pallas as pl
from jax.experimental.pallas import tpu as pltpu
from jax.sharding import Mesh
from jax.sharding import PartitionSpec as P

N = 4096
FINE = 32
COARSE = 1024
M = 256
ROWS = 8
DISTANCES = (4, 3, 5, 2, 6, 1, 7)
COL = ("col_0", "col_1")
PLANE_COL = ("plane", "col_0", "col_1")
HIGH = lax.Precision.HIGHEST
LIMIT = 20 << 20


def turns():
    turn = 2.0 * math.pi / N * (np.arange(16) - 8)[:, None] * np.arange(M)[None, :]
    tall = np.zeros((2, M, 128), np.float32)
    tall[0, :, :16] = np.cos(turn).T
    tall[1, :, :16] = np.sin(turn).T
    wide = np.stack([np.cos(turn), np.sin(turn)], axis=1)[:, :, None, :]
    return wide.astype(np.float32), tall


def base_kernel(out):
    lag = lax.broadcasted_iota(jnp.int32, (M, M), 0) - lax.broadcasted_iota(jnp.int32, (M, M), 1)
    size = jnp.abs(lag)
    angle = jnp.minimum(size, M - size).astype(jnp.float32) * (math.pi / M)
    scale = jnp.where((lag > 0) == (lax.rem(size, 2) == 0), math.pi / (16 * M), -math.pi / (16 * M))
    out[...] = jnp.where(lag == 0, 0.0, scale / jnp.where(lag == 0, 1.0, jnp.sin(angle)))


def matrices(base, wide, tall, k):
    lane = lax.broadcasted_iota(jnp.int32, (M, 128), 1)
    ca = jnp.sum(jnp.where(lane == k, tall[0], 0.0), axis=1, keepdims=True)
    sa = jnp.sum(jnp.where(lane == k, tall[1], 0.0), axis=1, keepdims=True)
    cb, sb = wide[k, 0], wide[k, 1]
    common = base[...]
    same = lax.broadcasted_iota(jnp.int32, (M, M), 0) == lax.broadcasted_iota(jnp.int32, (M, M), 1)
    middle = (k - 8).astype(jnp.float32) * (2.0 * math.pi / (16 * N))
    imag = common * (sa * cb - ca * sb) + jnp.where(same, middle, 0.0)
    return common * (ca * cb + sa * sb), jnp.where(k == 0, common, imag)


def vmem_call(kernel, outs, scratch=(), smem=0):
    def call(*args):
        specs = [pl.BlockSpec(memory_space=pltpu.SMEM)] * smem
        specs += [pl.BlockSpec(memory_space=pltpu.VMEM)] * (len(args) - smem)
        many = isinstance(outs, (list, tuple))
        out_specs = jax.tree.map(lambda _: pl.BlockSpec(memory_space=pltpu.VMEM), list(outs) if many else outs)
        return pl.pallas_call(
            kernel,
            out_shape=list(outs) if many else outs,
            in_specs=specs,
            out_specs=out_specs,
            scratch_shapes=list(scratch),
            compiler_params=pltpu.CompilerParams(vmem_limit_bytes=LIMIT),
        )(*args)

    return call


def near(values):
    return pltpu.with_memory_space_constraint(values, pltpu.VMEM)


def f32(*shape):
    return jax.ShapeDtypeStruct(shape, jnp.float32)


def real_dft(values):
    n = len(values)
    if n == 2:
        return [(values[0] + values[1], None), (values[0] - values[1], None)]
    even, odd = real_dft(values[0::2]), real_dft(values[1::2])
    half = n // 2
    out = [None] * (half + 1)
    out[0] = (even[0][0] + odd[0][0], None)
    out[half] = (even[0][0] - odd[0][0], None)
    for k in range(1, n // 4):
        angle = 2.0 * math.pi * k / n
        c, s = math.cos(angle), math.sin(angle)
        (er, ei), (orr, oi) = even[k], odd[k]
        if 2 * k * 4 == n:
            tr, ti = (orr + oi) * c, (oi - orr) * c
        else:
            tr, ti = orr * c + oi * s, oi * c - orr * s
        out[k] = (er + tr, ei + ti)
        out[half - k] = (er - tr, ti - ei)
    q = n // 4
    out[q] = (even[q][0], -odd[q][0])
    return out


def real_idft(spec):
    half = len(spec) - 1
    n = 2 * half
    if n == 2:
        return [spec[0][0] + spec[1][0], spec[0][0] - spec[1][0]]
    q = n // 4
    even, odd = [None] * (q + 1), [None] * (q + 1)
    even[0] = (spec[0][0] + spec[half][0], None)
    odd[0] = (spec[0][0] - spec[half][0], None)
    even[q] = (2.0 * spec[q][0], None)
    odd[q] = (-2.0 * spec[q][1], None)
    for k in range(1, q):
        angle = 2.0 * math.pi * k / n
        c, s = math.cos(angle), math.sin(angle)
        (ar, ai), (br, bi) = spec[k], spec[half - k]
        even[k] = (ar + br, ai - bi)
        dr, di = ar - br, ai + bi
        if 8 * k == n:
            odd[k] = ((dr - di) * c, (dr + di) * c)
        else:
            odd[k] = (dr * c - di * s, dr * s + di * c)
    out = [None] * n
    out[0::2] = real_idft(even)
    out[1::2] = real_idft(odd)
    return out


def lane_ids(rows):
    return lax.broadcasted_iota(jnp.int32, (rows, 128), 1)


def swap_lanes(four):
    group = lax.broadcasted_iota(jnp.int32, four[0].shape, 1) // 32
    low, even = group < 2, lax.rem(group, 2) == 0
    a, b, c, d = four
    a, c = jnp.where(low, a, pltpu.roll(c, 64, 1)), jnp.where(low, pltpu.roll(a, 64, 1), c)
    b, d = jnp.where(low, b, pltpu.roll(d, 64, 1)), jnp.where(low, pltpu.roll(b, 64, 1), d)
    a, b = jnp.where(even, a, pltpu.roll(b, 32, 1)), jnp.where(even, pltpu.roll(a, 96, 1), b)
    c, d = jnp.where(even, c, pltpu.roll(d, 32, 1)), jnp.where(even, pltpu.roll(c, 96, 1), d)
    return a, b, c, d


def pack_rows_kernel(row, *refs, count, step=32):
    vels, outs, held = refs[:count], refs[count : count + 8], refs[count + 8]

    def body(i, carry):
        rows = pl.ds(pl.multiple_of(i * step, step), step)
        later = pl.ds(pl.multiple_of(i * step + 256, step), step)
        for n, vel in enumerate(vels):
            for t in range(2):
                lanes = pl.ds(t * 128, 128)
                four = swap_lanes([vel[0, p, r, lanes] for r in (rows, later) for p in range(2)])
                for off in range(4):
                    held[4 * t + off, n, rows, :] = four[off]
        return carry

    lax.fori_loop(0, 256 // step, body, 0)
    for dist in range(ROWS):
        outs[dist][...] = held[lax.rem(row[0] + dist, ROWS)]


def pack_rows(row, velocity, comps):
    count = len(comps)
    whole = pl.BlockSpec((count, 256, 128), lambda i: (0, 0, 0))

    def one(c):
        return pl.BlockSpec((1, 2, 512, 256), lambda i: (c, 0, 0, 0))

    return pl.pallas_call(
        functools.partial(pack_rows_kernel, count=count),
        out_shape=[f32(count, 256, 128)] * ROWS,
        grid=(1,),
        in_specs=[pl.BlockSpec(memory_space=pltpu.SMEM)] + [one(c) for c in comps],
        out_specs=[whole] * ROWS,
        scratch_shapes=[pltpu.VMEM((ROWS, count, 256, 128), jnp.float32)],
        name="pack_rows",
        compiler_params=pltpu.CompilerParams(vmem_limit_bytes=LIMIT),
    )(row, *([velocity] * count))


def hold_blocks(row, blocks, held):
    for dist in range(ROWS):
        held[lax.rem(row[0] + dist, ROWS)] = blocks[dist][0]


def home_tiles(held, rows, t):
    four = swap_lanes([held[4 * t + off, rows, :] for off in range(4)])
    return {(half, p): four[2 * half + p] for half in range(2) for p in range(2)}


def send_blocks(blocks):
    got = [blocks[0]] + [None] * (ROWS - 1)
    for dist in DISTANCES:
        perm = [(i, (i + dist) % ROWS) for i in range(ROWS)]
        got[(ROWS - dist) % ROWS] = lax.ppermute(blocks[dist], "row", perm)
    return got


def spectral_x(tables, spec, res):
    def body(k, carry):
        lone = k == 0
        first, second = matrices(*tables, k)
        a = jnp.dot(first, spec[k], precision=HIGH)
        b = jnp.dot(second, spec[k], precision=HIGH)
        res[k, :, :128] = a[:, :128] - jnp.where(lone, 0.0, b[:, 128:])
        res[k, :, 128:] = jnp.where(lone, b[:, 128:], a[:, 128:] + b[:, :128])
        return carry

    lax.fori_loop(0, 8, body, 0, unroll=2)


STEP = 16


def store_spec(spec, freq, rows):
    for k in range(8):
        re, im = freq[k]
        spec[k, rows, :128] = re
        spec[k, rows, 128:] = freq[8][0] if k == 0 else im


def load_spec(res, rows):
    freq = [(res[k, rows, :128], res[k, rows, 128:]) for k in range(8)]
    return [(freq[0][0], None)] + freq[1:] + [(freq[0][1], None)]


def grad_v_kernel(*refs):
    tables, refs = refs[:3], refs[3:]
    blocks, outs, spec, res = refs[:8], refs[8:16], refs[16], refs[17]
    low = lane_ids(STEP) < 64

    def forward(i, carry):
        rows = pl.ds(pl.multiple_of(i * STEP, STEP), STEP)
        values = []
        for j in range(8):
            src = blocks[j][0, rows, :]
            values += [src, pltpu.roll(src, 64, 1)]
        store_spec(spec, real_dft(values), rows)
        return carry

    lax.fori_loop(0, 256 // STEP, forward, 0)
    spectral_x(tables, spec, res)

    def backward(i, carry):
        rows = pl.ds(pl.multiple_of(i * STEP, STEP), STEP)
        values = real_idft(load_spec(res, rows))
        for j in range(8):
            outs[j][0, rows, :] = jnp.where(low, values[2 * j], pltpu.roll(values[2 * j + 1], 64, 1))
        return carry

    lax.fori_loop(0, 256 // STEP, backward, 0)


X_SCRATCH = (pltpu.VMEM((8, 256, 256), jnp.float32), pltpu.VMEM((8, 256, 256), jnp.float32))


def grad_v(tables, blocks):
    return vmem_call(grad_v_kernel, [f32(1, 256, 128)] * 8, X_SCRATCH)(*tables, *blocks)


def stack_first_kernel(*refs):
    for j in range(8):
        refs[8][j] = refs[j][0]


def stack_first(blocks):
    one = pl.BlockSpec((1, 256, 128), lambda i: (0, 0, 0))
    return pl.pallas_call(
        stack_first_kernel,
        out_shape=f32(8, 256, 128),
        grid=(1,),
        in_specs=[one] * 8,
        out_specs=pl.BlockSpec((8, 256, 128), lambda i: (0, 0, 0)),
        name="stack_first",
        compiler_params=pltpu.CompilerParams(vmem_limit_bytes=LIMIT),
    )(*blocks)


def grad_uw_kernel(row, *refs):
    tables, refs = refs[:3], refs[3:]
    blocks, other, out, sums, spec, res = refs[:8], *refs[8:]
    lane = lane_ids(STEP)
    low = lane < 64
    first = lax.rem(lane // 32, 2) == 0

    def forward(i, carry):
        rows = pl.ds(pl.multiple_of(i * STEP, STEP), STEP)
        values = []
        for j in range(8):
            u, w = blocks[j][0, rows, :], blocks[j][1, rows, :]
            values += [jnp.where(low, u, pltpu.roll(w, 64, 1)), jnp.where(low, pltpu.roll(u, 64, 1), w)]
        store_spec(spec, real_dft(values), rows)
        return carry

    lax.fori_loop(0, 256 // STEP, forward, 0)
    spectral_x(tables, spec, res)

    def backward(i, carry):
        rows = pl.ds(pl.multiple_of(i * STEP, STEP), STEP)
        values = real_idft(load_spec(res, rows))
        totals = []
        for j in range(8):
            a, b = values[2 * j], values[2 * j + 1]
            u_x = jnp.where(low, a, pltpu.roll(b, 64, 1))
            w_x = jnp.where(low, pltpu.roll(a, 64, 1), b)
            diff = blocks[j][0, rows, :] - other[j, rows, :]
            u_z = 0.5 * jnp.where(first, pltpu.roll(diff, 96, 1), -pltpu.roll(diff, 32, 1))
            cross = u_z + w_x
            part = u_x * u_x + 0.5 * (cross * cross)
            out[lax.rem(row[0] + j, ROWS), rows, :] = part
            totals.append(carry[j] + part)
        return tuple(totals)

    zero = jnp.zeros((STEP, 128), jnp.float32)
    totals = lax.fori_loop(0, 256 // STEP, backward, (zero,) * 8)
    for j in range(8):
        sums[j : j + 1, :] = jnp.sum(totals[j], axis=0, keepdims=True)


def grad_uw(row, tables, other, blocks):
    outs = [f32(8, 256, 128), f32(8, 128)]
    return vmem_call(grad_uw_kernel, outs, X_SCRATCH, smem=1)(row, *tables, *blocks, other)


def grad_y_kernel(base, wide, tall, data, out, spec, res):
    tables = (base, wide, tall)

    def forward(i, carry):
        c = i // 16
        k = lax.rem(i // 8, 2)
        p = lax.rem(i // 4, 2)
        half = pl.ds(pl.multiple_of(lax.rem(i // 2, 2) * 8, 8), 8)
        lanes = pl.ds(pl.multiple_of(lax.rem(i, 2) * 128, 128), 128)
        rows = pl.multiple_of((i // 2) * 8, 8)
        freq = real_dft([data[k, b, c, p, half, lanes] for b in range(16)])
        for f in range(8):
            spec[f, pl.ds(rows, 8), lanes] = freq[f][0]
            spec[f, pl.ds(rows + 192, 8), lanes] = freq[8][0] if f == 0 else freq[f][1]
        return carry

    lax.fori_loop(0, 48, forward, 0)

    def middle(f, carry):
        lone = f == 0
        first, second = matrices(*tables, f)
        a = jnp.dot(spec[f], first, precision=HIGH)
        b = jnp.dot(spec[f], second, precision=HIGH)
        res[f, :192] = -a[:192] - jnp.where(lone, 0.0, b[192:])
        res[f, 192:] = jnp.where(lone, -b[192:], b[:192] - a[192:])
        return carry

    lax.fori_loop(0, 8, middle, 0, unroll=2)

    def backward(i, carry):
        k = i // 4
        half = pl.ds(pl.multiple_of(lax.rem(i // 2, 2) * 8, 8), 8)
        lanes = pl.ds(pl.multiple_of(lax.rem(i, 2) * 128, 128), 128)
        for p in range(2):

            def slope(c):
                start = pl.multiple_of(c * 64 + k * 32 + p * 16 + lax.rem(i // 2, 2) * 8, 8)
                freq = [(res[f, pl.ds(start, 8), lanes], res[f, pl.ds(start + 192, 8), lanes]) for f in range(8)]
                return real_idft([(freq[0][0], None)] + freq[1:] + [(freq[0][1], None)])

            def slope_z(c, b):
                gap = data[k, b, c, 1 - p, half, lanes] - data[1 - k, b, c, 1 - p, half, lanes]
                return gap * (0.5 if p == 0 else -0.5)

            for b, value in enumerate(slope(0)):
                out[k, b, 1, p, half, lanes] = value
            for b, value in enumerate(slope(1)):
                w_z = slope_z(2, b)
                out[k, b, 0, p, half, lanes] = value * value + w_z * w_z
            for b, value in enumerate(slope(2)):
                cross = slope_z(1, b) + value
                out[k, b, 0, p, half, lanes] += 0.5 * (cross * cross)
        return carry

    lax.fori_loop(0, 8, backward, 0)


def grad_y(tables, data):
    scratch = (pltpu.VMEM((8, 384, 256), jnp.float32), pltpu.VMEM((8, 384, 256), jnp.float32))
    return vmem_call(grad_y_kernel, f32(2, 16, 2, 2, 16, 256), scratch)(*tables, near(data))


def pack_cols_kernel(vel, out):
    def body(g, carry):
        start = pl.multiple_of(g * 16, 16)
        for c in range(3):
            for p in range(2):
                out[g, c, p] = vel[c, p, pl.ds(start, 16), :]
        return carry

    lax.fori_loop(0, 32, body, 0)


def partial_kernel(place, y_terms, x_sums, *refs):
    blocks, out, boxes, held = refs[:8], refs[8], refs[9], refs[10]
    hold_blocks(place, blocks, held)

    def body(i, carry):
        rows = pl.ds(pl.multiple_of(i * 16, 16), 16)
        for t in range(2):
            lanes = pl.ds(t * 128, 128)
            for (half, p), v_x in home_tiles(held, rows, t).items():
                g = i + 16 * half
                cross = y_terms[g, 1, p, :, lanes] + v_x
                value = y_terms[g, 0, p, :, lanes] + 0.5 * (cross * cross)
                out[p, pl.ds(pl.multiple_of(g * 16, 16), 16), lanes] = value
                carry = carry + value
        return carry

    total = lax.fori_loop(0, 16, body, jnp.zeros((16, 128), jnp.float32))
    down = lax.broadcasted_iota(jnp.int32, (8, 128), 0)
    mine = lax.broadcasted_iota(jnp.int32, (8, 128), 1) == place[1] // 4
    zero = jnp.zeros((8, 128), jnp.float32)
    found = jnp.where(down == place[0] // 2, jnp.sum(total), zero)
    for j in range(ROWS):
        box = lax.rem(place[0] + j, ROWS) // 2
        found = found + jnp.where(down == box, jnp.sum(x_sums[j : j + 1, :]), zero)
    boxes[...] = jnp.where(mine, found * (1.0 / (4 * COARSE * COARSE)), zero)


def final_kernel(part, held, out, boxes, lines):

    def body(a, carry):
        rows = pl.ds(pl.multiple_of(a * 32, 32), 32)
        for t in range(2):
            lanes = pl.ds(t * 128, 128)
            tiles = home_tiles(held, rows, t)
            for half in range(2):
                there = pl.ds(pl.multiple_of(a * 32 + 256 * half, 32), 32)
                first = part[0, there, lanes] + tiles[half, 0]
                second = part[1, there, lanes] + tiles[half, 1]
                out[0, there, lanes] = first
                out[1, there, lanes] = second
                total = (first + second).reshape(4, 8, 128).sum(axis=0)
                lines[a + 8 * half, :, lanes] = total
        return carry

    lax.fori_loop(0, 8, body, 0)
    cell = lax.broadcasted_iota(jnp.int32, (256, 128), 0) // FINE
    select = jnp.where(cell == lax.broadcasted_iota(jnp.int32, (256, 128), 1), 1.0 / (4 * FINE * FINE), 0.0)
    boxes[...] = jnp.dot(jnp.sum(lines[...], axis=1), select, precision=HIGH)


def whole_step(velocity):
    row = lax.axis_index("row")
    col = lax.axis_index(COL)
    row_arg = row.astype(jnp.int32).reshape(1)
    for_cols = vmem_call(pack_cols_kernel, f32(32, 3, 2, 16, 256))(velocity)
    lines = lax.all_to_all(for_cols, PLANE_COL, split_axis=0, concat_axis=0, tiled=True)
    v_blocks = pack_rows(row_arg, velocity, (1,))
    v_blocks = send_blocks(v_blocks)
    uw_blocks = pack_rows(row_arg, velocity, (0, 2))
    uw_blocks = send_blocks(uw_blocks)
    tables = (vmem_call(base_kernel, f32(M, M))(), *(jnp.asarray(a) for a in turns()))
    v_x = grad_v(tables, v_blocks)
    v_x = send_blocks(v_x)
    y_terms = grad_y(tables, lines.reshape(2, 16, 3, 2, 16, 256))
    y_terms = lax.all_to_all(
        y_terms.reshape(32, 2, 2, 16, 256), PLANE_COL, split_axis=0, concat_axis=0, tiled=True
    )
    other = stack_first(uw_blocks)
    other = lax.ppermute(other, "plane", [(0, 1), (1, 0)])
    x_terms, x_sums = grad_uw(row_arg, tables, other, uw_blocks)
    x_terms = lax.all_to_all(x_terms, "row", split_axis=0, concat_axis=0, tiled=True)
    held = pltpu.VMEM((ROWS, 256, 128), jnp.float32)
    place = jnp.stack([row, col]).astype(jnp.int32)
    part, coarse = vmem_call(partial_kernel, [f32(2, 512, 256), f32(8, 128)], (held,), smem=1)(
        place, near(y_terms), x_sums, *v_x
    )
    coarse = sum_of_four(coarse, "col_1", lambda i, n: (i + (2, 1, 3)[n]) % 4)
    coarse = sum_of_four(coarse, "col_0", lambda i, n: (i + (2, 1, 3)[n]) % 4)
    coarse = sum_of_four(coarse, ("plane", "row"), lambda i, n: i ^ (8, 1, 9)[n])
    coarse = sum_of_four(coarse, "row", lambda i, n: (i + (4, 2, 6)[n]) % 8)
    coarse = coarse[:4, :4]
    dissip, fine = vmem_call(
        final_kernel,
        [f32(2, 512, 256), f32(16, 128)],
        (pltpu.VMEM((16, 8, 256), jnp.float32),),
    )(part, near(x_terms))
    fine = (fine + lax.ppermute(fine, "plane", [(0, 1), (1, 0)]))[:, :8]
    return dissip, fine, coarse


def sum_of_four(values, axis, partner):
    size = lax.axis_size(axis)
    got = [lax.ppermute(values, axis, [(i, partner(i, n)) for i in range(size)]) for n in range(3)]
    return (values + got[0]) + (got[1] + got[2])


def solution(mesh):
    split = Mesh(
        mesh.devices.reshape(mesh.shape["plane"], mesh.shape["row"], 4, 4),
        ("plane", "row", "col_0", "col_1"),
    )
    in_specs = (P(None, "plane", "row", COL),)
    out_specs = (P("plane", "row", COL), P("row", COL), P())
    return jax.shard_map(whole_step, mesh=split, in_specs=in_specs, out_specs=out_specs, check_vma=False)
```

```python
import functools
import math

import jax
import jax.numpy as jnp
import numpy as np
from jax import lax
from jax.experimental import pallas as pl
from jax.experimental.pallas import tpu as pltpu
from jax.sharding import Mesh
from jax.sharding import PartitionSpec as P

N = 4096
FINE = 32
COARSE = 1024
M = 256
ROWS = 8
DISTANCES = (4, 3, 5, 2, 6, 1, 7)
COL = ("col_0", "col_1")
PLANE_COL = ("plane", "col_0", "col_1")
HIGH = lax.Precision.HIGHEST
LIMIT = 20 << 20


def turns():
    turn = 2.0 * math.pi / N * (np.arange(16) - 8)[:, None] * np.arange(M)[None, :]
    tall = np.zeros((2, M, 128), np.float32)
    tall[0, :, :16] = np.cos(turn).T
    tall[1, :, :16] = np.sin(turn).T
    wide = np.stack([np.cos(turn), np.sin(turn)], axis=1)[:, :, None, :]
    return wide.astype(np.float32), tall


def base_kernel(out):
    lag = lax.broadcasted_iota(jnp.int32, (M, M), 0) - lax.broadcasted_iota(jnp.int32, (M, M), 1)
    size = jnp.abs(lag)
    angle = jnp.minimum(size, M - size).astype(jnp.float32) * (math.pi / M)
    scale = jnp.where((lag > 0) == (lax.rem(size, 2) == 0), math.pi / (16 * M), -math.pi / (16 * M))
    out[...] = jnp.where(lag == 0, 0.0, scale / jnp.where(lag == 0, 1.0, jnp.sin(angle)))


def matrices(base, wide, tall, k):
    lane = lax.broadcasted_iota(jnp.int32, (M, 128), 1)
    ca = jnp.sum(jnp.where(lane == k, tall[0], 0.0), axis=1, keepdims=True)
    sa = jnp.sum(jnp.where(lane == k, tall[1], 0.0), axis=1, keepdims=True)
    cb, sb = wide[k, 0], wide[k, 1]
    common = base[...]
    same = lax.broadcasted_iota(jnp.int32, (M, M), 0) == lax.broadcasted_iota(jnp.int32, (M, M), 1)
    middle = (k - 8).astype(jnp.float32) * (2.0 * math.pi / (16 * N))
    imag = common * (sa * cb - ca * sb) + jnp.where(same, middle, 0.0)
    return common * (ca * cb + sa * sb), jnp.where(k == 0, common, imag)


def vmem_call(kernel, outs, scratch=(), smem=0):
    def call(*args):
        specs = [pl.BlockSpec(memory_space=pltpu.SMEM)] * smem
        specs += [pl.BlockSpec(memory_space=pltpu.VMEM)] * (len(args) - smem)
        many = isinstance(outs, (list, tuple))
        out_specs = jax.tree.map(lambda _: pl.BlockSpec(memory_space=pltpu.VMEM), list(outs) if many else outs)
        return pl.pallas_call(
            kernel,
            out_shape=list(outs) if many else outs,
            in_specs=specs,
            out_specs=out_specs,
            scratch_shapes=list(scratch),
            compiler_params=pltpu.CompilerParams(vmem_limit_bytes=LIMIT),
        )(*args)

    return call


def near(values):
    return pltpu.with_memory_space_constraint(values, pltpu.VMEM)


def far(values):
    return pltpu.with_memory_space_constraint(values, pltpu.HBM)


def f32_far(*shape):
    return pltpu.HBM(shape, jnp.float32)


def f32(*shape):
    return jax.ShapeDtypeStruct(shape, jnp.float32)


def real_dft(values):
    n = len(values)
    if n == 2:
        return [(values[0] + values[1], None), (values[0] - values[1], None)]
    even, odd = real_dft(values[0::2]), real_dft(values[1::2])
    half = n // 2
    out = [None] * (half + 1)
    out[0] = (even[0][0] + odd[0][0], None)
    out[half] = (even[0][0] - odd[0][0], None)
    for k in range(1, n // 4):
        angle = 2.0 * math.pi * k / n
        c, s = math.cos(angle), math.sin(angle)
        (er, ei), (orr, oi) = even[k], odd[k]
        if 2 * k * 4 == n:
            tr, ti = (orr + oi) * c, (oi - orr) * c
        else:
            tr, ti = orr * c + oi * s, oi * c - orr * s
        out[k] = (er + tr, ei + ti)
        out[half - k] = (er - tr, ti - ei)
    q = n // 4
    out[q] = (even[q][0], -odd[q][0])
    return out


def real_idft(spec):
    half = len(spec) - 1
    n = 2 * half
    if n == 2:
        return [spec[0][0] + spec[1][0], spec[0][0] - spec[1][0]]
    q = n // 4
    even, odd = [None] * (q + 1), [None] * (q + 1)
    even[0] = (spec[0][0] + spec[half][0], None)
    odd[0] = (spec[0][0] - spec[half][0], None)
    even[q] = (2.0 * spec[q][0], None)
    odd[q] = (-2.0 * spec[q][1], None)
    for k in range(1, q):
        angle = 2.0 * math.pi * k / n
        c, s = math.cos(angle), math.sin(angle)
        (ar, ai), (br, bi) = spec[k], spec[half - k]
        even[k] = (ar + br, ai - bi)
        dr, di = ar - br, ai + bi
        if 8 * k == n:
            odd[k] = ((dr - di) * c, (dr + di) * c)
        else:
            odd[k] = (dr * c - di * s, dr * s + di * c)
    out = [None] * n
    out[0::2] = real_idft(even)
    out[1::2] = real_idft(odd)
    return out


def lane_ids(rows):
    return lax.broadcasted_iota(jnp.int32, (rows, 128), 1)


def swap_lanes(four):
    group = lax.broadcasted_iota(jnp.int32, four[0].shape, 1) // 32
    low, even = group < 2, lax.rem(group, 2) == 0
    a, b, c, d = four
    a, c = jnp.where(low, a, pltpu.roll(c, 64, 1)), jnp.where(low, pltpu.roll(a, 64, 1), c)
    b, d = jnp.where(low, b, pltpu.roll(d, 64, 1)), jnp.where(low, pltpu.roll(b, 64, 1), d)
    a, b = jnp.where(even, a, pltpu.roll(b, 32, 1)), jnp.where(even, pltpu.roll(a, 96, 1), b)
    c, d = jnp.where(even, c, pltpu.roll(d, 32, 1)), jnp.where(even, pltpu.roll(c, 96, 1), d)
    return a, b, c, d


def pack_rows_kernel(row, *refs, count, step=32):
    vels, outs, held = refs[:count], refs[count : count + 8], refs[count + 8]

    def body(i, carry):
        rows = pl.ds(pl.multiple_of(i * step, step), step)
        later = pl.ds(pl.multiple_of(i * step + 256, step), step)
        for n, vel in enumerate(vels):
            for t in range(2):
                lanes = pl.ds(t * 128, 128)
                four = swap_lanes([vel[0, p, r, lanes] for r in (rows, later) for p in range(2)])
                for off in range(4):
                    held[4 * t + off, n, rows, :] = four[off]
        return carry

    lax.fori_loop(0, 256 // step, body, 0)
    for dist in range(ROWS):
        outs[dist][...] = held[lax.rem(row[0] + dist, ROWS)]


def pack_rows(row, velocity, comps):
    count = len(comps)
    whole = pl.BlockSpec((count, 256, 128), lambda i: (0, 0, 0))

    def one(c):
        return pl.BlockSpec((1, 2, 512, 256), lambda i: (c, 0, 0, 0))

    return pl.pallas_call(
        functools.partial(pack_rows_kernel, count=count),
        out_shape=[f32_far(count, 256, 128)] * ROWS,
        grid=(1,),
        in_specs=[pl.BlockSpec(memory_space=pltpu.SMEM)] + [one(c) for c in comps],
        out_specs=[whole] * ROWS,
        scratch_shapes=[pltpu.VMEM((ROWS, count, 256, 128), jnp.float32)],
        name="pack_rows",
        compiler_params=pltpu.CompilerParams(vmem_limit_bytes=LIMIT),
    )(row, *([velocity] * count))


def hold_blocks(row, blocks, held):
    for dist in range(ROWS):
        held[lax.rem(row[0] + dist, ROWS)] = blocks[dist][0]


def home_tiles(held, rows, t):
    four = swap_lanes([held[4 * t + off, rows, :] for off in range(4)])
    return {(half, p): four[2 * half + p] for half in range(2) for p in range(2)}


def send_blocks(blocks):
    got = [far(blocks[0])] + [None] * (ROWS - 1)
    for dist in DISTANCES:
        perm = [(i, (i + dist) % ROWS) for i in range(ROWS)]
        got[(ROWS - dist) % ROWS] = lax.ppermute(blocks[dist], "row", perm)
    return got


def spectral_x(tables, spec, res):
    def body(k, carry):
        lone = k == 0
        first, second = matrices(*tables, k)
        a = jnp.dot(first, spec[k], precision=HIGH)
        b = jnp.dot(second, spec[k], precision=HIGH)
        res[k, :, :128] = a[:, :128] - jnp.where(lone, 0.0, b[:, 128:])
        res[k, :, 128:] = jnp.where(lone, b[:, 128:], a[:, 128:] + b[:, :128])
        return carry

    lax.fori_loop(0, 8, body, 0, unroll=2)


STEP = 16


def store_spec(spec, freq, rows):
    for k in range(8):
        re, im = freq[k]
        spec[k, rows, :128] = re
        spec[k, rows, 128:] = freq[8][0] if k == 0 else im


def load_spec(res, rows):
    freq = [(res[k, rows, :128], res[k, rows, 128:]) for k in range(8)]
    return [(freq[0][0], None)] + freq[1:] + [(freq[0][1], None)]


def grad_v_kernel(*refs):
    tables, refs = refs[:3], refs[3:]
    blocks, outs, spec, res = refs[:8], refs[8:16], refs[16], refs[17]
    low = lane_ids(STEP) < 64

    def forward(i, carry):
        rows = pl.ds(pl.multiple_of(i * STEP, STEP), STEP)
        values = []
        for j in range(8):
            src = blocks[j][0, rows, :]
            values += [src, pltpu.roll(src, 64, 1)]
        store_spec(spec, real_dft(values), rows)
        return carry

    lax.fori_loop(0, 256 // STEP, forward, 0)
    spectral_x(tables, spec, res)

    def backward(i, carry):
        rows = pl.ds(pl.multiple_of(i * STEP, STEP), STEP)
        values = real_idft(load_spec(res, rows))
        for j in range(8):
            outs[j][0, rows, :] = jnp.where(low, values[2 * j], pltpu.roll(values[2 * j + 1], 64, 1))
        return carry

    lax.fori_loop(0, 256 // STEP, backward, 0)


X_SCRATCH = (pltpu.VMEM((8, 256, 256), jnp.float32), pltpu.VMEM((8, 256, 256), jnp.float32))


def grad_v(tables, blocks):
    return vmem_call(grad_v_kernel, [f32_far(1, 256, 128)] * 8, X_SCRATCH)(*tables, *blocks)


def stack_first_kernel(*refs):
    for j in range(8):
        refs[8][j] = refs[j][0]


def stack_first(blocks):
    one = pl.BlockSpec((1, 256, 128), lambda i: (0, 0, 0))
    return pl.pallas_call(
        stack_first_kernel,
        out_shape=f32(8, 256, 128),
        grid=(1,),
        in_specs=[one] * 8,
        out_specs=pl.BlockSpec((8, 256, 128), lambda i: (0, 0, 0)),
        name="stack_first",
        compiler_params=pltpu.CompilerParams(vmem_limit_bytes=LIMIT),
    )(*blocks)


def grad_uw_kernel(row, *refs):
    tables, refs = refs[:3], refs[3:]
    blocks, other, out, sums, spec, res = refs[:8], *refs[8:]
    lane = lane_ids(STEP)
    low = lane < 64
    first = lax.rem(lane // 32, 2) == 0

    def forward(i, carry):
        rows = pl.ds(pl.multiple_of(i * STEP, STEP), STEP)
        values = []
        for j in range(8):
            u, w = blocks[j][0, rows, :], blocks[j][1, rows, :]
            values += [jnp.where(low, u, pltpu.roll(w, 64, 1)), jnp.where(low, pltpu.roll(u, 64, 1), w)]
        store_spec(spec, real_dft(values), rows)
        return carry

    lax.fori_loop(0, 256 // STEP, forward, 0)
    spectral_x(tables, spec, res)

    def backward(i, carry):
        rows = pl.ds(pl.multiple_of(i * STEP, STEP), STEP)
        values = real_idft(load_spec(res, rows))
        totals = []
        for j in range(8):
            a, b = values[2 * j], values[2 * j + 1]
            u_x = jnp.where(low, a, pltpu.roll(b, 64, 1))
            w_x = jnp.where(low, pltpu.roll(a, 64, 1), b)
            diff = blocks[j][0, rows, :] - other[j, rows, :]
            u_z = 0.5 * jnp.where(first, pltpu.roll(diff, 96, 1), -pltpu.roll(diff, 32, 1))
            cross = u_z + w_x
            part = u_x * u_x + 0.5 * (cross * cross)
            out[lax.rem(row[0] + j, ROWS), rows, :] = part
            totals.append(carry[j] + part)
        return tuple(totals)

    zero = jnp.zeros((STEP, 128), jnp.float32)
    totals = lax.fori_loop(0, 256 // STEP, backward, (zero,) * 8)
    for j in range(8):
        sums[j : j + 1, :] = jnp.sum(totals[j], axis=0, keepdims=True)


def grad_uw(row, tables, other, blocks):
    outs = [f32(8, 256, 128), f32(8, 128)]
    return vmem_call(grad_uw_kernel, outs, X_SCRATCH, smem=1)(row, *tables, *blocks, other)


def grad_y_kernel(base, wide, tall, data, out, spec, res):
    tables = (base, wide, tall)

    def forward(i, carry):
        c = i // 16
        k = lax.rem(i // 8, 2)
        p = lax.rem(i // 4, 2)
        half = pl.ds(pl.multiple_of(lax.rem(i // 2, 2) * 8, 8), 8)
        lanes = pl.ds(pl.multiple_of(lax.rem(i, 2) * 128, 128), 128)
        rows = pl.multiple_of((i // 2) * 8, 8)
        freq = real_dft([data[k, b, c, p, half, lanes] for b in range(16)])
        for f in range(8):
            spec[f, pl.ds(rows, 8), lanes] = freq[f][0]
            spec[f, pl.ds(rows + 192, 8), lanes] = freq[8][0] if f == 0 else freq[f][1]
        return carry

    lax.fori_loop(0, 48, forward, 0)

    def middle(f, carry):
        lone = f == 0
        first, second = matrices(*tables, f)
        a = jnp.dot(spec[f], first, precision=HIGH)
        b = jnp.dot(spec[f], second, precision=HIGH)
        res[f, :192] = -a[:192] - jnp.where(lone, 0.0, b[192:])
        res[f, 192:] = jnp.where(lone, -b[192:], b[:192] - a[192:])
        return carry

    lax.fori_loop(0, 8, middle, 0, unroll=2)

    def backward(i, carry):
        k = i // 4
        half = pl.ds(pl.multiple_of(lax.rem(i // 2, 2) * 8, 8), 8)
        lanes = pl.ds(pl.multiple_of(lax.rem(i, 2) * 128, 128), 128)
        for p in range(2):

            def slope(c):
                start = pl.multiple_of(c * 64 + k * 32 + p * 16 + lax.rem(i // 2, 2) * 8, 8)
                freq = [(res[f, pl.ds(start, 8), lanes], res[f, pl.ds(start + 192, 8), lanes]) for f in range(8)]
                return real_idft([(freq[0][0], None)] + freq[1:] + [(freq[0][1], None)])

            def slope_z(c, b):
                gap = data[k, b, c, 1 - p, half, lanes] - data[1 - k, b, c, 1 - p, half, lanes]
                return gap * (0.5 if p == 0 else -0.5)

            for b, value in enumerate(slope(0)):
                out[k, b, 1, p, half, lanes] = value
            for b, value in enumerate(slope(1)):
                w_z = slope_z(2, b)
                out[k, b, 0, p, half, lanes] = value * value + w_z * w_z
            for b, value in enumerate(slope(2)):
                cross = slope_z(1, b) + value
                out[k, b, 0, p, half, lanes] += 0.5 * (cross * cross)
        return carry

    lax.fori_loop(0, 8, backward, 0)


def grad_y(tables, data):
    scratch = (pltpu.VMEM((8, 384, 256), jnp.float32), pltpu.VMEM((8, 384, 256), jnp.float32))
    return vmem_call(grad_y_kernel, f32(2, 16, 2, 2, 16, 256), scratch)(*tables, near(data))


def pack_cols_kernel(vel, out):
    def body(g, carry):
        start = pl.multiple_of(g * 16, 16)
        for c in range(3):
            for p in range(2):
                out[g, c, p] = vel[c, p, pl.ds(start, 16), :]
        return carry

    lax.fori_loop(0, 32, body, 0)


def partial_kernel(place, y_terms, x_sums, *refs):
    blocks, out, boxes, held = refs[:8], refs[8], refs[9], refs[10]
    hold_blocks(place, blocks, held)

    def body(i, carry):
        rows = pl.ds(pl.multiple_of(i * 16, 16), 16)
        for t in range(2):
            lanes = pl.ds(t * 128, 128)
            for (half, p), v_x in home_tiles(held, rows, t).items():
                g = i + 16 * half
                cross = y_terms[g, 1, p, :, lanes] + v_x
                value = y_terms[g, 0, p, :, lanes] + 0.5 * (cross * cross)
                out[p, pl.ds(pl.multiple_of(g * 16, 16), 16), lanes] = value
                carry = carry + value
        return carry

    total = lax.fori_loop(0, 16, body, jnp.zeros((16, 128), jnp.float32))
    down = lax.broadcasted_iota(jnp.int32, (8, 128), 0)
    mine = lax.broadcasted_iota(jnp.int32, (8, 128), 1) == place[1] // 4
    zero = jnp.zeros((8, 128), jnp.float32)
    found = jnp.where(down == place[0] // 2, jnp.sum(total), zero)
    for j in range(ROWS):
        box = lax.rem(place[0] + j, ROWS) // 2
        found = found + jnp.where(down == box, jnp.sum(x_sums[j : j + 1, :]), zero)
    boxes[...] = jnp.where(mine, found * (1.0 / (4 * COARSE * COARSE)), zero)


def final_kernel(part, held, out, boxes, lines):

    def body(a, carry):
        rows = pl.ds(pl.multiple_of(a * 32, 32), 32)
        for t in range(2):
            lanes = pl.ds(t * 128, 128)
            tiles = home_tiles(held, rows, t)
            for half in range(2):
                there = pl.ds(pl.multiple_of(a * 32 + 256 * half, 32), 32)
                first = part[0, there, lanes] + tiles[half, 0]
                second = part[1, there, lanes] + tiles[half, 1]
                out[0, there, lanes] = first
                out[1, there, lanes] = second
                total = (first + second).reshape(4, 8, 128).sum(axis=0)
                lines[a + 8 * half, :, lanes] = total
        return carry

    lax.fori_loop(0, 8, body, 0)
    cell = lax.broadcasted_iota(jnp.int32, (256, 128), 0) // FINE
    select = jnp.where(cell == lax.broadcasted_iota(jnp.int32, (256, 128), 1), 1.0 / (4 * FINE * FINE), 0.0)
    boxes[...] = jnp.dot(jnp.sum(lines[...], axis=1), select, precision=HIGH)


def whole_step(velocity):
    row = lax.axis_index("row")
    col = lax.axis_index(COL)
    row_arg = row.astype(jnp.int32).reshape(1)
    for_cols = vmem_call(pack_cols_kernel, f32(32, 3, 2, 16, 256))(velocity)
    lines = lax.all_to_all(for_cols, PLANE_COL, split_axis=0, concat_axis=0, tiled=True)
    v_blocks = pack_rows(row_arg, velocity, (1,))
    v_blocks = send_blocks(v_blocks)
    uw_blocks = pack_rows(row_arg, velocity, (0, 2))
    uw_blocks = send_blocks(uw_blocks)
    tables = (vmem_call(base_kernel, f32(M, M))(), *(jnp.asarray(a) for a in turns()))
    v_x = grad_v(tables, v_blocks)
    v_x = send_blocks(v_x)
    y_terms = grad_y(tables, lines.reshape(2, 16, 3, 2, 16, 256))
    y_terms = lax.all_to_all(
        y_terms.reshape(32, 2, 2, 16, 256), PLANE_COL, split_axis=0, concat_axis=0, tiled=True
    )
    other = stack_first(uw_blocks)
    other = lax.ppermute(other, "plane", [(0, 1), (1, 0)])
    x_terms, x_sums = grad_uw(row_arg, tables, other, uw_blocks)
    x_terms = lax.all_to_all(x_terms, "row", split_axis=0, concat_axis=0, tiled=True)
    held = pltpu.VMEM((ROWS, 256, 128), jnp.float32)
    place = jnp.stack([row, col]).astype(jnp.int32)
    part, coarse = vmem_call(partial_kernel, [f32_far(2, 512, 256), f32(8, 128)], (held,), smem=1)(
        place, near(y_terms), x_sums, *v_x
    )
    coarse = sum_of_four(coarse, "col_1", lambda i, n: (i + (2, 1, 3)[n]) % 4)
    coarse = sum_of_four(coarse, "col_0", lambda i, n: (i + (2, 1, 3)[n]) % 4)
    coarse = sum_of_four(coarse, ("plane", "row"), lambda i, n: i ^ (8, 1, 9)[n])
    coarse = sum_of_four(coarse, "row", lambda i, n: (i + (4, 2, 6)[n]) % 8)
    coarse = coarse[:4, :4]
    dissip, fine = vmem_call(
        final_kernel,
        [f32(2, 512, 256), f32(16, 128)],
        (pltpu.VMEM((16, 8, 256), jnp.float32),),
    )(far(part), near(x_terms))
    fine = (fine + lax.ppermute(fine, "plane", [(0, 1), (1, 0)]))[:, :8]
    return dissip, fine, coarse


def sum_of_four(values, axis, partner):
    size = lax.axis_size(axis)
    got = [lax.ppermute(values, axis, [(i, partner(i, n)) for i in range(size)]) for n in range(3)]
    return (values + got[0]) + (got[1] + got[2])


def solution(mesh):
    split = Mesh(
        mesh.devices.reshape(mesh.shape["plane"], mesh.shape["row"], 4, 4),
        ("plane", "row", "col_0", "col_1"),
    )
    in_specs = (P(None, "plane", "row", COL),)
    out_specs = (P("plane", "row", COL), P("row", COL), P())
    return jax.shard_map(whole_step, mesh=split, in_specs=in_specs, out_specs=out_specs, check_vma=False)
```

```python
import functools
import math

import jax
import jax.numpy as jnp
import numpy as np
from jax import lax
from jax.experimental import pallas as pl
from jax.experimental.pallas import tpu as pltpu
from jax.sharding import Mesh
from jax.sharding import PartitionSpec as P

N = 4096
FINE = 32
COARSE = 1024
M = 256
ROWS = 8
DISTANCES = (4, 3, 5, 2, 6, 1, 7)
COL = ("col_0", "col_1")
PLANE_COL = ("plane", "col_0", "col_1")
HIGH = lax.Precision.HIGHEST
LIMIT = 20 << 20


def turns():
    turn = 2.0 * math.pi / N * (np.arange(16) - 8)[:, None] * np.arange(M)[None, :]
    tall = np.zeros((2, M, 128), np.float32)
    tall[0, :, :16] = np.cos(turn).T
    tall[1, :, :16] = np.sin(turn).T
    wide = np.stack([np.cos(turn), np.sin(turn)], axis=1)[:, :, None, :]
    return wide.astype(np.float32), tall


def base_kernel(out):
    lag = lax.broadcasted_iota(jnp.int32, (M, M), 0) - lax.broadcasted_iota(jnp.int32, (M, M), 1)
    size = jnp.abs(lag)
    angle = jnp.minimum(size, M - size).astype(jnp.float32) * (math.pi / M)
    scale = jnp.where((lag > 0) == (lax.rem(size, 2) == 0), math.pi / (16 * M), -math.pi / (16 * M))
    out[...] = jnp.where(lag == 0, 0.0, scale / jnp.where(lag == 0, 1.0, jnp.sin(angle)))


def matrices(base, wide, tall, k):
    lane = lax.broadcasted_iota(jnp.int32, (M, 128), 1)
    ca = jnp.sum(jnp.where(lane == k, tall[0], 0.0), axis=1, keepdims=True)
    sa = jnp.sum(jnp.where(lane == k, tall[1], 0.0), axis=1, keepdims=True)
    cb, sb = wide[k, 0], wide[k, 1]
    common = base[...]
    same = lax.broadcasted_iota(jnp.int32, (M, M), 0) == lax.broadcasted_iota(jnp.int32, (M, M), 1)
    middle = (k - 8).astype(jnp.float32) * (2.0 * math.pi / (16 * N))
    imag = common * (sa * cb - ca * sb) + jnp.where(same, middle, 0.0)
    return common * (ca * cb + sa * sb), jnp.where(k == 0, common, imag)


def vmem_call(kernel, outs, scratch=(), smem=0):
    def call(*args):
        specs = [pl.BlockSpec(memory_space=pltpu.SMEM)] * smem
        specs += [pl.BlockSpec(memory_space=pltpu.VMEM)] * (len(args) - smem)
        many = isinstance(outs, (list, tuple))
        out_specs = jax.tree.map(lambda _: pl.BlockSpec(memory_space=pltpu.VMEM), list(outs) if many else outs)
        return pl.pallas_call(
            kernel,
            out_shape=list(outs) if many else outs,
            in_specs=specs,
            out_specs=out_specs,
            scratch_shapes=list(scratch),
            compiler_params=pltpu.CompilerParams(vmem_limit_bytes=LIMIT),
        )(*args)

    return call


def near(values):
    return pltpu.with_memory_space_constraint(values, pltpu.VMEM)


def far(values):
    return pltpu.with_memory_space_constraint(values, pltpu.HBM)


def f32_far(*shape):
    return pltpu.HBM(shape, jnp.float32)


def f32(*shape):
    return jax.ShapeDtypeStruct(shape, jnp.float32)


def real_dft(values):
    n = len(values)
    if n == 2:
        return [(values[0] + values[1], None), (values[0] - values[1], None)]
    even, odd = real_dft(values[0::2]), real_dft(values[1::2])
    half = n // 2
    out = [None] * (half + 1)
    out[0] = (even[0][0] + odd[0][0], None)
    out[half] = (even[0][0] - odd[0][0], None)
    for k in range(1, n // 4):
        angle = 2.0 * math.pi * k / n
        c, s = math.cos(angle), math.sin(angle)
        (er, ei), (orr, oi) = even[k], odd[k]
        if 2 * k * 4 == n:
            tr, ti = (orr + oi) * c, (oi - orr) * c
        else:
            tr, ti = orr * c + oi * s, oi * c - orr * s
        out[k] = (er + tr, ei + ti)
        out[half - k] = (er - tr, ti - ei)
    q = n // 4
    out[q] = (even[q][0], -odd[q][0])
    return out


def real_idft(spec):
    half = len(spec) - 1
    n = 2 * half
    if n == 2:
        return [spec[0][0] + spec[1][0], spec[0][0] - spec[1][0]]
    q = n // 4
    even, odd = [None] * (q + 1), [None] * (q + 1)
    even[0] = (spec[0][0] + spec[half][0], None)
    odd[0] = (spec[0][0] - spec[half][0], None)
    even[q] = (2.0 * spec[q][0], None)
    odd[q] = (-2.0 * spec[q][1], None)
    for k in range(1, q):
        angle = 2.0 * math.pi * k / n
        c, s = math.cos(angle), math.sin(angle)
        (ar, ai), (br, bi) = spec[k], spec[half - k]
        even[k] = (ar + br, ai - bi)
        dr, di = ar - br, ai + bi
        if 8 * k == n:
            odd[k] = ((dr - di) * c, (dr + di) * c)
        else:
            odd[k] = (dr * c - di * s, dr * s + di * c)
    out = [None] * n
    out[0::2] = real_idft(even)
    out[1::2] = real_idft(odd)
    return out


def lane_ids(rows):
    return lax.broadcasted_iota(jnp.int32, (rows, 128), 1)


def swap_lanes(four):
    group = lax.broadcasted_iota(jnp.int32, four[0].shape, 1) // 32
    low, even = group < 2, lax.rem(group, 2) == 0
    a, b, c, d = four
    a, c = jnp.where(low, a, pltpu.roll(c, 64, 1)), jnp.where(low, pltpu.roll(a, 64, 1), c)
    b, d = jnp.where(low, b, pltpu.roll(d, 64, 1)), jnp.where(low, pltpu.roll(b, 64, 1), d)
    a, b = jnp.where(even, a, pltpu.roll(b, 32, 1)), jnp.where(even, pltpu.roll(a, 96, 1), b)
    c, d = jnp.where(even, c, pltpu.roll(d, 32, 1)), jnp.where(even, pltpu.roll(c, 96, 1), d)
    return a, b, c, d


def pack_rows_kernel(row, *refs, count, step=32):
    vels, outs, held = refs[:count], refs[count : count + 8], refs[count + 8]

    def body(i, carry):
        rows = pl.ds(pl.multiple_of(i * step, step), step)
        later = pl.ds(pl.multiple_of(i * step + 256, step), step)
        for n, vel in enumerate(vels):
            for t in range(2):
                lanes = pl.ds(t * 128, 128)
                four = swap_lanes([vel[0, p, r, lanes] for r in (rows, later) for p in range(2)])
                for off in range(4):
                    held[4 * t + off, n, rows, :] = four[off]
        return carry

    lax.fori_loop(0, 256 // step, body, 0)
    for dist in range(ROWS):
        outs[dist][...] = held[lax.rem(row[0] + dist, ROWS)]


def pack_rows(row, velocity, comps):
    count = len(comps)
    whole = pl.BlockSpec((count, 256, 128), lambda i: (0, 0, 0))

    def one(c):
        return pl.BlockSpec((1, 2, 512, 256), lambda i: (c, 0, 0, 0))

    return pl.pallas_call(
        functools.partial(pack_rows_kernel, count=count),
        out_shape=[f32_far(count, 256, 128)] * ROWS,
        grid=(1,),
        in_specs=[pl.BlockSpec(memory_space=pltpu.SMEM)] + [one(c) for c in comps],
        out_specs=[whole] * ROWS,
        scratch_shapes=[pltpu.VMEM((ROWS, count, 256, 128), jnp.float32)],
        name="pack_rows",
        compiler_params=pltpu.CompilerParams(vmem_limit_bytes=LIMIT),
    )(row, *([velocity] * count))


def hold_blocks(row, blocks, held):
    for dist in range(ROWS):
        held[lax.rem(row[0] + dist, ROWS)] = blocks[dist][0]


def home_tiles(held, rows, t):
    four = swap_lanes([held[4 * t + off, rows, :] for off in range(4)])
    return {(half, p): four[2 * half + p] for half in range(2) for p in range(2)}


def send_blocks(blocks):
    got = [far(blocks[0])] + [None] * (ROWS - 1)
    for dist in DISTANCES:
        perm = [(i, (i + dist) % ROWS) for i in range(ROWS)]
        got[(ROWS - dist) % ROWS] = lax.ppermute(blocks[dist], "row", perm)
    return got


def spectral_x(tables, spec, res):
    def body(k, carry):
        lone = k == 0
        first, second = matrices(*tables, k)
        a = jnp.dot(first, spec[k], precision=HIGH)
        b = jnp.dot(second, spec[k], precision=HIGH)
        res[k, :, :128] = a[:, :128] - jnp.where(lone, 0.0, b[:, 128:])
        res[k, :, 128:] = jnp.where(lone, b[:, 128:], a[:, 128:] + b[:, :128])
        return carry

    lax.fori_loop(0, 8, body, 0, unroll=2)


STEP = 16


def store_spec(spec, freq, rows):
    for k in range(8):
        re, im = freq[k]
        spec[k, rows, :128] = re
        spec[k, rows, 128:] = freq[8][0] if k == 0 else im


def load_spec(res, rows):
    freq = [(res[k, rows, :128], res[k, rows, 128:]) for k in range(8)]
    return [(freq[0][0], None)] + freq[1:] + [(freq[0][1], None)]


def grad_v_kernel(*refs):
    tables, refs = refs[:3], refs[3:]
    blocks, outs, spec, res = refs[:8], refs[8:16], refs[16], refs[17]
    low = lane_ids(STEP) < 64

    def forward(i, carry):
        rows = pl.ds(pl.multiple_of(i * STEP, STEP), STEP)
        values = []
        for j in range(8):
            src = blocks[j][0, rows, :]
            values += [src, pltpu.roll(src, 64, 1)]
        store_spec(spec, real_dft(values), rows)
        return carry

    lax.fori_loop(0, 256 // STEP, forward, 0)
    spectral_x(tables, spec, res)

    def backward(i, carry):
        rows = pl.ds(pl.multiple_of(i * STEP, STEP), STEP)
        values = real_idft(load_spec(res, rows))
        for j in range(8):
            outs[j][0, rows, :] = jnp.where(low, values[2 * j], pltpu.roll(values[2 * j + 1], 64, 1))
        return carry

    lax.fori_loop(0, 256 // STEP, backward, 0)


X_SCRATCH = (pltpu.VMEM((8, 256, 256), jnp.float32), pltpu.VMEM((8, 256, 256), jnp.float32))


def grad_v(tables, blocks):
    return vmem_call(grad_v_kernel, [f32_far(1, 256, 128)] * 8, X_SCRATCH)(*tables, *blocks)


def stack_first_kernel(*refs):
    for j in range(8):
        refs[8][j] = refs[j][0]


def stack_first(blocks):
    one = pl.BlockSpec((1, 256, 128), lambda i: (0, 0, 0))
    return pl.pallas_call(
        stack_first_kernel,
        out_shape=f32(8, 256, 128),
        grid=(1,),
        in_specs=[one] * 8,
        out_specs=pl.BlockSpec((8, 256, 128), lambda i: (0, 0, 0)),
        name="stack_first",
        compiler_params=pltpu.CompilerParams(vmem_limit_bytes=LIMIT),
    )(*blocks)


def grad_uw_kernel(row, *refs):
    tables, refs = refs[:3], refs[3:]
    blocks, other, out, sums, spec, res = refs[:8], *refs[8:]
    lane = lane_ids(STEP)
    low = lane < 64
    first = lax.rem(lane // 32, 2) == 0

    def forward(i, carry):
        rows = pl.ds(pl.multiple_of(i * STEP, STEP), STEP)
        values = []
        for j in range(8):
            u, w = blocks[j][0, rows, :], blocks[j][1, rows, :]
            values += [jnp.where(low, u, pltpu.roll(w, 64, 1)), jnp.where(low, pltpu.roll(u, 64, 1), w)]
        store_spec(spec, real_dft(values), rows)
        return carry

    lax.fori_loop(0, 256 // STEP, forward, 0)
    spectral_x(tables, spec, res)

    def backward(i, carry):
        rows = pl.ds(pl.multiple_of(i * STEP, STEP), STEP)
        values = real_idft(load_spec(res, rows))
        totals = []
        for j in range(8):
            a, b = values[2 * j], values[2 * j + 1]
            u_x = jnp.where(low, a, pltpu.roll(b, 64, 1))
            w_x = jnp.where(low, pltpu.roll(a, 64, 1), b)
            diff = blocks[j][0, rows, :] - other[j, rows, :]
            u_z = 0.5 * jnp.where(first, pltpu.roll(diff, 96, 1), -pltpu.roll(diff, 32, 1))
            cross = u_z + w_x
            part = u_x * u_x + 0.5 * (cross * cross)
            out[lax.rem(row[0] + j, ROWS), rows, :] = part
            totals.append(carry[j] + part)
        return tuple(totals)

    zero = jnp.zeros((STEP, 128), jnp.float32)
    totals = lax.fori_loop(0, 256 // STEP, backward, (zero,) * 8)
    for j in range(8):
        sums[j : j + 1, :] = jnp.sum(totals[j], axis=0, keepdims=True)


def grad_uw(row, tables, other, blocks):
    outs = [f32(8, 256, 128), f32(8, 128)]
    return vmem_call(grad_uw_kernel, outs, X_SCRATCH, smem=1)(row, *tables, *blocks, other)


def grad_y_kernel(base, wide, tall, data, out, spec, res):
    tables = (base, wide, tall)

    def forward(i, carry):
        c = i // 16
        k = lax.rem(i // 8, 2)
        p = lax.rem(i // 4, 2)
        half = pl.ds(pl.multiple_of(lax.rem(i // 2, 2) * 8, 8), 8)
        lanes = pl.ds(pl.multiple_of(lax.rem(i, 2) * 128, 128), 128)
        rows = pl.multiple_of((i // 2) * 8, 8)
        freq = real_dft([data[k, b, c, p, half, lanes] for b in range(16)])
        for f in range(8):
            spec[f, pl.ds(rows, 8), lanes] = freq[f][0]
            spec[f, pl.ds(rows + 192, 8), lanes] = freq[8][0] if f == 0 else freq[f][1]
        return carry

    lax.fori_loop(0, 48, forward, 0)

    def middle(f, carry):
        lone = f == 0
        first, second = matrices(*tables, f)
        a = jnp.dot(spec[f], first, precision=HIGH)
        b = jnp.dot(spec[f], second, precision=HIGH)
        res[f, :192] = -a[:192] - jnp.where(lone, 0.0, b[192:])
        res[f, 192:] = jnp.where(lone, -b[192:], b[:192] - a[192:])
        return carry

    lax.fori_loop(0, 8, middle, 0, unroll=2)

    def backward(i, carry):
        k = i // 4
        half = pl.ds(pl.multiple_of(lax.rem(i // 2, 2) * 8, 8), 8)
        lanes = pl.ds(pl.multiple_of(lax.rem(i, 2) * 128, 128), 128)
        for p in range(2):

            def slope(c):
                start = pl.multiple_of(c * 64 + k * 32 + p * 16 + lax.rem(i // 2, 2) * 8, 8)
                freq = [(res[f, pl.ds(start, 8), lanes], res[f, pl.ds(start + 192, 8), lanes]) for f in range(8)]
                return real_idft([(freq[0][0], None)] + freq[1:] + [(freq[0][1], None)])

            def slope_z(c, b):
                gap = data[k, b, c, 1 - p, half, lanes] - data[1 - k, b, c, 1 - p, half, lanes]
                return gap * (0.5 if p == 0 else -0.5)

            for b, value in enumerate(slope(0)):
                out[k, b, 1, p, half, lanes] = value
            for b, value in enumerate(slope(1)):
                w_z = slope_z(2, b)
                out[k, b, 0, p, half, lanes] = value * value + w_z * w_z
            for b, value in enumerate(slope(2)):
                cross = slope_z(1, b) + value
                out[k, b, 0, p, half, lanes] += 0.5 * (cross * cross)
        return carry

    lax.fori_loop(0, 8, backward, 0)


def grad_y(tables, data):
    scratch = (pltpu.VMEM((8, 384, 256), jnp.float32), pltpu.VMEM((8, 384, 256), jnp.float32))
    return vmem_call(grad_y_kernel, f32(2, 16, 2, 2, 16, 256), scratch)(*tables, near(data))


def pack_cols_kernel(vel, out):
    for g in range(8):
        for c in range(3):
            for p in range(2):
                out[g, c, p] = vel[c, p, 16 * g : 16 * g + 16, :]


def pack_cols(velocity):
    return pl.pallas_call(
        pack_cols_kernel,
        out_shape=f32_far(32, 3, 2, 16, 256),
        grid=(4,),
        in_specs=[pl.BlockSpec((3, 2, 128, 256), lambda i: (0, 0, i, 0))],
        out_specs=pl.BlockSpec((8, 3, 2, 16, 256), lambda i: (i, 0, 0, 0, 0)),
        compiler_params=pltpu.CompilerParams(vmem_limit_bytes=LIMIT),
        name="pack_cols",
    )(far(velocity))


def partial_kernel(place, y_terms, x_sums, *refs):
    blocks, out, boxes, held = refs[:8], refs[8], refs[9], refs[10]
    hold_blocks(place, blocks, held)

    def body(i, carry):
        rows = pl.ds(pl.multiple_of(i * 16, 16), 16)
        for t in range(2):
            lanes = pl.ds(t * 128, 128)
            for (half, p), v_x in home_tiles(held, rows, t).items():
                g = i + 16 * half
                cross = y_terms[g, 1, p, :, lanes] + v_x
                value = y_terms[g, 0, p, :, lanes] + 0.5 * (cross * cross)
                out[p, pl.ds(pl.multiple_of(g * 16, 16), 16), lanes] = value
                carry = carry + value
        return carry

    total = lax.fori_loop(0, 16, body, jnp.zeros((16, 128), jnp.float32))
    down = lax.broadcasted_iota(jnp.int32, (8, 128), 0)
    mine = lax.broadcasted_iota(jnp.int32, (8, 128), 1) == place[1] // 4
    zero = jnp.zeros((8, 128), jnp.float32)
    found = jnp.where(down == place[0] // 2, jnp.sum(total), zero)
    for j in range(ROWS):
        box = lax.rem(place[0] + j, ROWS) // 2
        found = found + jnp.where(down == box, jnp.sum(x_sums[j : j + 1, :]), zero)
    boxes[...] = jnp.where(mine, found * (1.0 / (4 * COARSE * COARSE)), zero)


def final_kernel(part, held, out, boxes, lines):

    def body(a, carry):
        rows = pl.ds(pl.multiple_of(a * 32, 32), 32)
        for t in range(2):
            lanes = pl.ds(t * 128, 128)
            tiles = home_tiles(held, rows, t)
            for half in range(2):
                there = pl.ds(pl.multiple_of(a * 32 + 256 * half, 32), 32)
                first = part[0, there, lanes] + tiles[half, 0]
                second = part[1, there, lanes] + tiles[half, 1]
                out[0, there, lanes] = first
                out[1, there, lanes] = second
                total = (first + second).reshape(4, 8, 128).sum(axis=0)
                lines[a + 8 * half, :, lanes] = total
        return carry

    lax.fori_loop(0, 8, body, 0)
    cell = lax.broadcasted_iota(jnp.int32, (256, 128), 0) // FINE
    select = jnp.where(cell == lax.broadcasted_iota(jnp.int32, (256, 128), 1), 1.0 / (4 * FINE * FINE), 0.0)
    boxes[...] = jnp.dot(jnp.sum(lines[...], axis=1), select, precision=HIGH)


def whole_step(velocity):
    row = lax.axis_index("row")
    col = lax.axis_index(COL)
    row_arg = row.astype(jnp.int32).reshape(1)
    for_cols = pack_cols(velocity)
    lines = lax.all_to_all(for_cols, PLANE_COL, split_axis=0, concat_axis=0, tiled=True)
    v_blocks = pack_rows(row_arg, velocity, (1,))
    v_blocks = send_blocks(v_blocks)
    uw_blocks = pack_rows(row_arg, velocity, (0, 2))
    uw_blocks = send_blocks(uw_blocks)
    tables = (vmem_call(base_kernel, f32(M, M))(), *(jnp.asarray(a) for a in turns()))
    v_x = grad_v(tables, v_blocks)
    v_x = send_blocks(v_x)
    y_terms = grad_y(tables, lines.reshape(2, 16, 3, 2, 16, 256))
    y_terms = lax.all_to_all(
        y_terms.reshape(32, 2, 2, 16, 256), PLANE_COL, split_axis=0, concat_axis=0, tiled=True
    )
    other = stack_first(uw_blocks)
    other = lax.ppermute(other, "plane", [(0, 1), (1, 0)])
    x_terms, x_sums = grad_uw(row_arg, tables, other, uw_blocks)
    x_terms = lax.all_to_all(x_terms, "row", split_axis=0, concat_axis=0, tiled=True)
    held = pltpu.VMEM((ROWS, 256, 128), jnp.float32)
    place = jnp.stack([row, col]).astype(jnp.int32)
    part, coarse = vmem_call(partial_kernel, [f32_far(2, 512, 256), f32(8, 128)], (held,), smem=1)(
        place, near(y_terms), x_sums, *v_x
    )
    coarse = sum_of_four(coarse, "col_1", lambda i, n: (i + (2, 1, 3)[n]) % 4)
    coarse = sum_of_four(coarse, "col_0", lambda i, n: (i + (2, 1, 3)[n]) % 4)
    coarse = sum_of_four(coarse, ("plane", "row"), lambda i, n: i ^ (8, 1, 9)[n])
    coarse = sum_of_four(coarse, "row", lambda i, n: (i + (4, 2, 6)[n]) % 8)
    coarse = coarse[:4, :4]
    dissip, fine = vmem_call(
        final_kernel,
        [f32(2, 512, 256), f32(16, 128)],
        (pltpu.VMEM((16, 8, 256), jnp.float32),),
    )(far(part), near(x_terms))
    fine = (fine + lax.ppermute(fine, "plane", [(0, 1), (1, 0)]))[:, :8]
    return dissip, fine, coarse


def sum_of_four(values, axis, partner):
    size = lax.axis_size(axis)
    got = [lax.ppermute(values, axis, [(i, partner(i, n)) for i in range(size)]) for n in range(3)]
    return (values + got[0]) + (got[1] + got[2])


def solution(mesh):
    split = Mesh(
        mesh.devices.reshape(mesh.shape["plane"], mesh.shape["row"], 4, 4),
        ("plane", "row", "col_0", "col_1"),
    )
    in_specs = (P(None, "plane", "row", COL),)
    out_specs = (P("plane", "row", COL), P("row", COL), P())
    return jax.shard_map(whole_step, mesh=split, in_specs=in_specs, out_specs=out_specs, check_vma=False)
```
